256 devices in a mesh: lat: 32 (over z_hi, y, core), chan: 8 (over z_lo, x).
Axes of the slice: x: 4, y: 4, z: 8 (z_hi: 4, z_lo: 2; z = z_hi * 2 + z_lo), core: 2. Of those that a mesh axis runs over, the one named last changes fastest.
Arguments:
- fields: float32 [256, 900, 768], P(('lat', 'chan')), may hold values from -6 to 6
- first_gain: float32 [768], replicated, may hold values from 0.5 to 1.5
- first_shift: float32 [768], replicated, may hold values from -1.5 to 1.5
- filter_one: float32 [8, 2, 96, 96], P('chan'), may hold values from -0.4375 to 0.4375
- filter_one_bias: float32 [8, 2, 96], P('chan'), may hold values from -2.5 to 2.5
- filter_two: float32 [8, 2, 96, 96], P('chan'), may hold values from -0.4375 to 0.4375
- filter_two_bias: float32 [8, 2, 96], P('chan'), may hold values from -2.5 to 2.5
- second_gain: float32 [768], replicated, may hold values from 0.5 to 1.5
- second_shift: float32 [768], replicated, may hold values from -1.5 to 1.5
- dense_weights: bfloat16 [3072, 2, 768], P(('lat', 'chan')), may hold values from -0.21875 to 0.21875
- dense_bias: bfloat16 [3072], P(('lat', 'chan')), may hold values from -2.5 to 2.5
- output_bias: float32 [768], replicated, may hold values from -1.5 to 1.5
Outputs:
- block_output: float32 [256, 900, 768], P(('lat', 'chan'))
The draws below stay inside these ranges and needn't reach their ends.
All inputs are finite; a program needn't handle non-finite values.
Results may differ from the reference program's by a relative error of at most 0.0025.
Values may be sent and summed in bfloat16 or wider, within the bound.
No kernel may reach another device: no remote copies, remote signals or barrier semaphores. Data moves between devices by JAX's collectives and lax.ppermute only.
A program may use at most 128 MiB of HBM per device.

```python
import jax
import jax.numpy as jnp
from jax import lax

C = 768
NB = 8
BS = 96
FF = 3072
W = 900
KW = 256
H = 256


def block_levels(own_key, extent, split, least, largest):
    level = 1.0
    for position, blocks in split:
        steps = jax.random.uniform(jax.random.fold_in(jax.random.fold_in(own_key, 6), position), (blocks,), jnp.float32, least / len(split), largest / len(split))
        level = level * jnp.repeat(jnp.exp(steps), extent[position] // blocks).reshape((-1,) + (1,) * (len(extent) - 1 - position))
    return level


def normal_values(own_key, shape, spread, reach, split=(), dtype=jnp.bfloat16):
    gain = block_levels(own_key, shape, split, -0.22, 0.18) if split else 1.0
    drawn = jax.random.normal(own_key, shape, jnp.float32) * spread * gain
    return jnp.minimum(jnp.maximum(drawn, -reach), reach).astype(dtype)


def setup_inputs(seed: int = 0) -> dict:
    seeds = jax.random.split(jax.random.key(seed), 13)
    fields = normal_values(seeds[0], (H, W, C), 1.0, 6.0, ((0, 256),), jnp.float32)
    first_gain = jnp.clip(1.0 + 0.1 * jax.random.normal(seeds[1], (C,), jnp.float32), 0.5, 1.5)
    first_shift = normal_values(seeds[2], (C,), 0.3, 1.5, (), jnp.float32)
    filter_one = normal_values(seeds[3], (NB, 2, BS, BS), (2 * BS) ** -0.5, 0.4375, ((0, 8),), jnp.float32)
    filter_one_bias = normal_values(seeds[4], (NB, 2, BS), 0.5, 2.5, ((0, 8),), jnp.float32)
    filter_two = normal_values(seeds[5], (NB, 2, BS, BS), (2 * BS) ** -0.5, 0.4375, ((0, 8),), jnp.float32)
    filter_two_bias = normal_values(seeds[6], (NB, 2, BS), 0.5, 2.5, ((0, 8),), jnp.float32)
    second_gain = jnp.clip(1.0 + 0.1 * jax.random.normal(seeds[7], (C,), jnp.float32), 0.5, 1.5)
    second_shift = normal_values(seeds[8], (C,), 0.3, 1.5, (), jnp.float32)
    dense_weights = normal_values(seeds[9], (FF, 2, C), C ** -0.5, 0.21875, ((0, 256),))
    dense_bias = normal_values(seeds[10], (FF,), 0.5, 2.5, ((0, 256),))
    output_bias = normal_values(seeds[11], (C,), 0.3, 1.5, (), jnp.float32)
    return {"fields": fields, "first_gain": first_gain, "first_shift": first_shift, "filter_one": filter_one, "filter_one_bias": filter_one_bias, "filter_two": filter_two, "filter_two_bias": filter_two_bias, "second_gain": second_gain, "second_shift": second_shift, "dense_weights": dense_weights, "dense_bias": dense_bias, "output_bias": output_bias}


exact_mode = lax.Precision.HIGHEST
norm_eps = 1e-05
shrink_level = 0.01

def layer_norm(values, gain_terms, shift_terms):
    mean_value = lax.optimization_barrier(jnp.mean(values, axis=-1, keepdims=True))
    centered = values - mean_value
    variance = lax.optimization_barrier(jnp.mean(centered * centered, axis=-1, keepdims=True))
    return centered * lax.rsqrt(variance + norm_eps) * gain_terms + shift_terms

def complex_layer(real_part, imag_part, weight, bias_terms):
    real_weight = weight[:, 0]
    imag_weight = weight[:, 1]
    out_real = jnp.einsum('hkni,nio->hkno', real_part, real_weight, precision=exact_mode) - jnp.einsum('hkni,nio->hkno', imag_part, imag_weight, precision=exact_mode) + bias_terms[:, 0]
    out_imag = jnp.einsum('hkni,nio->hkno', imag_part, real_weight, precision=exact_mode) + jnp.einsum('hkni,nio->hkno', real_part, imag_weight, precision=exact_mode) + bias_terms[:, 1]
    return (out_real, out_imag)

def soft_shrink(values):
    return jnp.sign(values) * jnp.maximum(jnp.abs(values) - shrink_level, 0.0)

def reference(fields, first_gain, first_shift, filter_one, filter_one_bias, filter_two, filter_two_bias, second_gain, second_shift, dense_weights, dense_bias, output_bias):
    normed_in = layer_norm(fields, first_gain, first_shift)
    lon_modes = jnp.fft.rfft(normed_in, axis=1, norm='ortho')[:, :KW, :]
    spectrum = jnp.fft.fft(lon_modes, axis=0, norm='ortho')
    real_part = jnp.real(spectrum).reshape(H, KW, NB, BS)
    imag_part = jnp.imag(spectrum).reshape(H, KW, NB, BS)
    real_part, imag_part = complex_layer(real_part, imag_part, filter_one, filter_one_bias)
    real_part = jnp.maximum(real_part, 0.0)
    imag_part = jnp.maximum(imag_part, 0.0)
    real_part, imag_part = complex_layer(real_part, imag_part, filter_two, filter_two_bias)
    real_part = soft_shrink(real_part)
    imag_part = soft_shrink(imag_part)
    mixed_modes = (real_part + 1j * imag_part).reshape(H, KW, C)
    lat_back = jnp.fft.ifft(mixed_modes, axis=0, norm='ortho')
    padded = jnp.pad(lat_back, ((0, 0), (0, W // 2 + 1 - KW), (0, 0)))
    filtered = jnp.fft.irfft(padded, n=W, axis=1, norm='ortho') + normed_in
    summed = filtered + fields

    def dense_row(row_values):
        row_normed = layer_norm(row_values, second_gain, second_shift).astype(jnp.bfloat16)
        pre_act = lax.dot_general(row_normed, dense_weights[:, 0, :], (((1,), (1,)), ((), ())), preferred_element_type=jnp.float32) + dense_bias.astype(jnp.float32)
        hidden = jax.nn.gelu(pre_act, approximate=False).astype(jnp.bfloat16)
        dense_out = jnp.dot(hidden, dense_weights[:, 1, :], preferred_element_type=jnp.float32)
        return row_values + (dense_out + output_bias)
    return lax.map(dense_row, summed)
```

```python
import functools

import jax
import jax.numpy as jnp
import numpy as np
from jax import lax
from jax.experimental import pallas as pl
from jax.experimental.pallas import tpu as pltpu
from jax.sharding import PartitionSpec as P

W = 900
WP = 1024
KW = 256
H = 256
C = 768
BS = 96
NB = 8
TILE = 304
ROWS = 3 * TILE
norm_eps = 1e-05
shrink_level = 0.01
AXES = ("lat", "chan")
bf16 = jnp.bfloat16
f32 = jnp.float32


def split_table(values):
    high = values.astype(np.float32).astype(jnp.bfloat16)
    low = (values - high.astype(np.float64)).astype(np.float32).astype(jnp.bfloat16)
    return high, low


def lon_tables():
    k = np.arange(KW)[:, None]
    w = np.arange(W)[None, :]
    angle = 2 * np.pi * (k * w % W) / W
    forward = np.zeros((KW, 2, WP))
    forward[:, 0, :W] = np.cos(angle)
    forward[:, 1, :W] = -np.sin(angle)
    forward = forward.reshape(2 * KW, WP) * W**-0.5
    factor = np.where(k == 0, 1.0, 2.0)
    backward = np.zeros((ROWS, KW, 2))
    backward[:W, :, 0] = (np.cos(angle) * factor).T
    backward[:W, :, 1] = (-np.sin(angle) * factor).T
    backward = backward.reshape(ROWS, 2 * KW) * W**-0.5
    return split_table(forward), split_table(backward)


def lat_tables():
    m = np.arange(H)[:, None]
    h = np.arange(H)[None, :]
    angle = 2 * np.pi * (m * h % H) / H
    cos, sin = np.cos(angle), np.sin(angle)
    forward = np.zeros((2, H, H, 2))
    forward[0, :, :, 0] = cos
    forward[0, :, :, 1] = sin
    forward[1, :, :, 0] = -sin
    forward[1, :, :, 1] = cos
    forward = forward.reshape(2 * H, 2 * H) * H**-0.5
    return split_table(forward), split_table(forward.T)


def dot(a, b):
    return jnp.dot(a, b, preferred_element_type=f32)


def split(x):
    high = x.astype(bf16)
    return high, (x - high.astype(f32)).astype(bf16)


def row_norm(parts, gain, shift):
    count = len(parts) * 128
    mean = jnp.sum(functools.reduce(jnp.add, parts), axis=-1, keepdims=True) / count
    centered = [p - mean for p in parts]
    square = functools.reduce(jnp.add, [c * c for c in centered])
    scale = lax.rsqrt(jnp.sum(square, axis=-1, keepdims=True) / count + norm_eps)
    return [
        c * scale * gain[:, 128 * j : 128 * j + 128] + shift[:, 128 * j : 128 * j + 128]
        for j, c in enumerate(centered)
    ]


def lon_kernel(x_ref, gain_ref, shift_ref, th_ref, tl_ref, modes_ref, base_ref, zh, zl):
    gain = gain_ref[...]
    shift = shift_ref[...]
    for start in range(0, W, 240):
        n = min(240, W - start)
        parts = [x_ref[pl.ds(6 * start + j, n, stride=6), :] for j in range(6)]
        normed = row_norm(parts, gain, shift)
        for j in range(6):
            lanes = slice(128 * j, 128 * j + 128)
            base_ref[start : start + n, lanes] = normed[j] + parts[j]
            high, low = split(normed[j])
            zh[start : start + n, lanes] = high
            zl[start : start + n, lanes] = low
    zh[W:WP, :] = jnp.zeros((WP - W, C), bf16)
    zl[W:WP, :] = jnp.zeros((WP - W, C), bf16)
    base_ref[W:ROWS, :] = jnp.zeros((ROWS - W, C), f32)
    modes = dot(th_ref[...], zh[...]) + dot(th_ref[...], zl[...]) + dot(tl_ref[...], zh[...])
    modes_ref[...] = modes.astype(bf16)


def pack_kernel(one_ref, one_bias_ref, two_ref, two_bias_ref, out_ref):
    for i, (w_ref, b_ref) in enumerate(((one_ref, one_bias_ref), (two_ref, two_bias_ref))):
        real, imag = w_ref[0], w_ref[1]
        top = jnp.concatenate([real, imag], axis=1)
        bottom = jnp.concatenate([-imag, real], axis=1)
        bias = jnp.concatenate([b_ref[0:1], b_ref[1:2]], axis=1)
        high = bias.astype(bf16).astype(f32)
        rows = lax.broadcasted_iota(jnp.int32, (16, 2 * BS), 0)
        tail = jnp.where(rows == 0, high, jnp.where(rows == 1, bias - high, 0.0))
        out_ref[i] = jnp.concatenate([top, bottom, tail], axis=0).astype(bf16)


def mode_kernel(own_ref, x_ref, fh_ref, fl_ref, gh_ref, gl_ref, *refs):
    w_refs, out_ref, w_all, zh, zl = refs[:NB], refs[NB], refs[NB + 1], refs[NB + 2], refs[NB + 3]
    for slot in range(NB):
        w_all[slot] = w_refs[slot][...]
    x = x_ref[...]
    y = dot(fh_ref[...], x) + dot(fl_ref[...], x)
    own = own_ref[0]

    def layer(values, slot, i):
        high, low = split(values)
        weight = w_all[slot, i, 0 : 2 * BS, :]
        bias = w_all[slot, i, 2 * BS : 2 * BS + 16, :].astype(f32)
        return dot(high, weight) + dot(low, weight) + (bias[0:1] + bias[1:2])

    outs = []
    for b in range(NB):
        slot = jnp.bitwise_xor(own, b)
        lanes = slice(BS * b, BS * b + BS)
        values = jnp.concatenate([y[:H, lanes], y[H:, lanes]], axis=1)
        first = jnp.maximum(layer(values, slot, 0), 0.0)
        second = layer(first, slot, 1)
        outs.append(second - jnp.clip(second, -shrink_level, shrink_level))
    for part in range(2):
        joined = jnp.concatenate([o[:, BS * part : BS * part + BS] for o in outs], axis=1)
        high, low = split(joined)
        zh[H * part : H * part + H, :] = high
        zl[H * part : H * part + H, :] = low
    back = dot(gh_ref[...], zh[...]) + dot(gh_ref[...], zl[...]) + dot(gl_ref[...], zh[...])
    out_ref[...] = back.astype(bf16)


def back_kernel(x_ref, th_ref, tl_ref, base_ref, gain_ref, shift_ref, bias_ref, sum_ref, norm_ref):
    gain = gain_ref[...]
    shift = shift_ref[...]
    bias = bias_ref[...]
    x = x_ref[...]
    for t in range(3):
        rows = slice(TILE * t, TILE * t + TILE)
        total = dot(th_ref[rows, :], x) + dot(tl_ref[rows, :], x) + base_ref[rows, :]
        parts = [total[:, 128 * j : 128 * j + 128] for j in range(6)]
        normed = row_norm(parts, gain, shift)
        norm_ref[rows, :] = jnp.concatenate(normed, axis=1).astype(bf16)
        sum_ref[rows, :] = total + bias


def gelu(x):
    return 0.5 * x * (1.0 + lax.erf(x * 0.7071067811865476))


def mlp_body(x_ref, acc_ref, w_refs, store):
    def tile(t, carry):
        rows = pl.ds(pl.multiple_of(t * TILE, 16), TILE)
        x = x_ref[rows, :]
        acc = acc_ref[rows, :]
        for pair in ((w_refs[0], w_refs[1]), (w_refs[2], w_refs[3])):
            w1 = jnp.concatenate([w[q, 0:BS, :] for w in pair for q in range(4)], axis=0)
            w2 = jnp.concatenate([w[q, BS : 2 * BS, :] for w in pair for q in range(4)], axis=0)
            bias = jnp.concatenate(
                [w[q, 2 * BS : 2 * BS + 16, :].astype(f32)[0:1, 0:BS] for w in pair for q in range(4)], axis=1
            )
            for c in range(3):
                span = slice(256 * c, 256 * c + 256)
                pre = lax.dot_general(x, w1[span], (((1,), (1,)), ((), ())), preferred_element_type=f32)
                hidden = gelu(pre + bias[:, span]).astype(bf16)
                acc = acc + dot(hidden, w2[span])
        store(t, rows, acc)
        return carry

    lax.fori_loop(0, 3, tile, 0)


def mlp_half(x_ref, acc_ref, w0, w1, w2, w3, out_ref):
    def store(t, rows, acc):
        out_ref[rows, :] = acc

    mlp_body(x_ref, acc_ref, (w0, w1, w2, w3), store)


def mlp_last(x_ref, acc_ref, w0, w1, w2, w3, out_ref, total):
    def store(t, rows, acc):
        total[rows, :] = acc

    mlp_body(x_ref, acc_ref, (w0, w1, w2, w3), store)
    for start in range(0, W, 240):
        n = min(240, W - start)
        for j in range(6):
            out_ref[pl.ds(6 * start + j, n, stride=6), :] = total[start : start + n, 128 * j : 128 * j + 128]


def vmem(n):
    return [pl.BlockSpec(memory_space=pltpu.VMEM)] * n


params = pltpu.CompilerParams(vmem_limit_bytes=56 * 2**20)


def place(index):
    lat, chan = divmod(index, 8)
    zh, rest = divmod(lat, 8)
    y, core = divmod(rest, 2)
    zl, x = divmod(chan, 4)
    return x, y, zh * 2 + zl, core


def index_of(x, y, z, core):
    return ((z // 2 * 4 + y) * 2 + core) * 8 + z % 2 * 4 + x


def moves(step):
    return [(d, index_of(*step(*place(d)))) for d in range(256)]


def z_moves(n):
    return moves(lambda x, y, z, c: (x, y, (z + n) % 8, c))


def near_moves(n):
    return moves(lambda x, y, z, c: (x, (y + n) % 4, z, c) if c == 0 else ((x + n) % 4, y, z, c))


def far_moves(n):
    return moves(lambda x, y, z, c: ((x + n) % 4, y, z, c) if c == 0 else (x, (y + n) % 4, z, c))


core_moves = moves(lambda x, y, z, c: (x, y, z, 1 - c))


def block_moves(bits):
    return [(d, d // 8 * 8 + ((d % 8) ^ bits)) for d in range(256)]


def per_device(
    fields,
    first_gain,
    first_shift,
    filter_one,
    filter_one_bias,
    filter_two,
    filter_two_bias,
    second_gain,
    second_shift,
    dense_weights,
    dense_bias,
    output_bias,
):
    (lon_h, lon_l), (back_h, back_l) = lon_tables()
    (lat_h, lat_l), (tal_h, tal_l) = lat_tables()
    shape = jax.ShapeDtypeStruct

    bias_rows = jnp.pad(dense_bias.reshape(1, 1, 12), ((0, 0), (0, 1), (0, C - 12)))
    shard = jnp.concatenate([dense_weights, bias_rows], axis=0)
    shards = [shard] + [lax.ppermute(shard, AXES, z_moves(n)) for n in (1, -1, 2, -2, 3, -3, 4)]

    packed = pl.pallas_call(
        pack_kernel,
        out_shape=shape((2, 2 * BS + 16, 2 * BS), bf16),
        in_specs=vmem(4),
        out_specs=vmem(1)[0],
        compiler_params=params,
        name="pack",
    )(filter_one[0], filter_one_bias[0], filter_two[0], filter_two_bias[0])
    filters = [packed] + [lax.ppermute(packed, AXES, block_moves(b)) for b in range(1, 8)]

    modes, base = pl.pallas_call(
        lon_kernel,
        out_shape=(shape((2 * KW, C), bf16), shape((ROWS, C), f32)),
        in_specs=vmem(5),
        out_specs=tuple(vmem(2)),
        scratch_shapes=[pltpu.VMEM((WP, C), bf16), pltpu.VMEM((WP, C), bf16)],
        compiler_params=params,
        name="lon",
    )(fields.reshape(6 * W, 128), first_gain[None], first_shift[None], lon_h, lon_l)

    stacked = jnp.stack(shards)
    rows_in = stacked[:, :12, 0, :].reshape(BS, C)
    rows_out = stacked[:, :12, 1, :].reshape(BS, C)
    bias_row = jnp.pad(stacked[:, 12, 0, :12].reshape(1, BS), ((0, 15), (0, C - BS)))
    block = jnp.concatenate([rows_in, rows_out, bias_row], axis=0)
    near = [block] + [lax.ppermute(block, AXES, near_moves(n)) for n in (1, -1, 2)]

    moved = lax.all_to_all(modes.reshape(256, 2, C), AXES, split_axis=0, concat_axis=0, tiled=True)

    group = jnp.stack(near)
    far = [group] + [lax.ppermute(group, AXES, far_moves(n)) for n in (1, -1, 2)]

    own = lax.axis_index("chan").astype(jnp.int32).reshape(1)
    mixed = pl.pallas_call(
        mode_kernel,
        out_shape=shape((2 * H, C), bf16),
        in_specs=[pl.BlockSpec(memory_space=pltpu.SMEM)] + vmem(5 + NB),
        out_specs=vmem(1)[0],
        scratch_shapes=[
            pltpu.VMEM((NB, 2, 2 * BS + 16, 2 * BS), bf16),
            pltpu.VMEM((2 * H, C), bf16),
            pltpu.VMEM((2 * H, C), bf16),
        ],
        compiler_params=params,
        name="mode",
    )(own, moved.reshape(2 * H, C), lat_h, lat_l, tal_h, tal_l, *filters)

    returned = lax.all_to_all(mixed.reshape(256, 2, C), AXES, split_axis=0, concat_axis=0, tiled=True)
    other = [lax.ppermute(g, AXES, core_moves) for g in far]

    summed, normed = pl.pallas_call(
        back_kernel,
        out_shape=(shape((ROWS, C), f32), shape((ROWS, C), bf16)),
        in_specs=vmem(7),
        out_specs=tuple(vmem(2)),
        compiler_params=params,
        name="back",
    )(returned.reshape(2 * KW, C), back_h, back_l, base, second_gain[None], second_shift[None], output_bias[None])

    half = pl.pallas_call(
        mlp_half,
        out_shape=shape((ROWS, C), f32),
        in_specs=vmem(6),
        out_specs=vmem(1)[0],
        compiler_params=params,
        name="mlp_half",
    )(normed, summed, *far)
    out = pl.pallas_call(
        mlp_last,
        out_shape=shape((6 * W, 128), f32),
        in_specs=vmem(6),
        out_specs=vmem(1)[0],
        scratch_shapes=[pltpu.VMEM((ROWS, C), f32)],
        compiler_params=params,
        name="mlp_last",
    )(normed, half, *other)
    return out.reshape(1, W, C)


def solution(mesh):
    placed = (
        P(("lat", "chan"), None, None),
        P(),
        P(),
        P("chan", None, None, None),
        P("chan", None, None),
        P("chan", None, None, None),
        P("chan", None, None),
        P(),
        P(),
        P(("lat", "chan"), None, None),
        P(("lat", "chan")),
        P(),
    )
    return jax.shard_map(
        per_device,
        mesh=mesh,
        in_specs=placed,
        out_specs=P(("lat", "chan"), None, None),
        check_vma=False,
    )
```

```python
import functools

import jax
import jax.numpy as jnp
import numpy as np
from jax import lax
from jax.experimental import pallas as pl
from jax.experimental.pallas import tpu as pltpu
from jax.sharding import Mesh
from jax.sharding import PartitionSpec as P


W = 900
WP = 1024
KW = 256
H = 256
C = 768
BS = 96
NB = 8
TILE = 304
ROWS = 3 * TILE
norm_eps = 1e-05
shrink_level = 0.01
AXES = ("zh", "y", "co", "zl", "x")
bf16 = jnp.bfloat16
f32 = jnp.float32


def split_table(values):
    high = values.astype(np.float32).astype(jnp.bfloat16)
    low = (values - high.astype(np.float64)).astype(np.float32).astype(jnp.bfloat16)
    return high, low


def lon_tables():
    k = np.arange(KW)[:, None]
    w = np.arange(W)[None, :]
    angle = 2 * np.pi * (k * w % W) / W
    forward = np.zeros((KW, 2, WP))
    forward[:, 0, :W] = np.cos(angle)
    forward[:, 1, :W] = -np.sin(angle)
    forward = forward.reshape(2 * KW, WP) * W**-0.5
    factor = np.where(k == 0, 1.0, 2.0)
    backward = np.zeros((ROWS, KW, 2))
    backward[:W, :, 0] = (np.cos(angle) * factor).T
    backward[:W, :, 1] = (-np.sin(angle) * factor).T
    backward = backward.reshape(ROWS, 2 * KW) * W**-0.5
    return split_table(forward), split_table(backward)


def lat_tables():
    m = np.arange(H)[:, None]
    h = np.arange(H)[None, :]
    angle = 2 * np.pi * (m * h % H) / H
    cos, sin = np.cos(angle), np.sin(angle)
    forward = np.zeros((2, H, H, 2))
    forward[0, :, :, 0] = cos
    forward[0, :, :, 1] = sin
    forward[1, :, :, 0] = -sin
    forward[1, :, :, 1] = cos
    forward = forward.reshape(2 * H, 2 * H) * H**-0.5
    return split_table(forward), split_table(forward.T)


def dot(a, b):
    return jnp.dot(a, b, preferred_element_type=f32)


def split(x):
    high = x.astype(bf16)
    return high, (x - high.astype(f32)).astype(bf16)


def row_norm(parts, gain, shift):
    count = len(parts) * 128
    mean = jnp.sum(functools.reduce(jnp.add, parts), axis=-1, keepdims=True) / count
    centered = [p - mean for p in parts]
    square = functools.reduce(jnp.add, [c * c for c in centered])
    scale = lax.rsqrt(jnp.sum(square, axis=-1, keepdims=True) / count + norm_eps)
    return [
        c * scale * gain[j : j + 1, :] + shift[j : j + 1, :]
        for j, c in enumerate(centered)
    ]


def lon_kernel(x_ref, gain_ref, shift_ref, th_ref, tl_ref, modes_ref, base_ref, zh, zl):
    gain = gain_ref[...]
    shift = shift_ref[...]
    for start in range(0, W, 240):
        n = min(240, W - start)
        parts = [x_ref[pl.ds(6 * start + j, n, stride=6), :] for j in range(6)]
        normed = row_norm(parts, gain, shift)
        for j in range(6):
            lanes = slice(128 * j, 128 * j + 128)
            base_ref[start : start + n, lanes] = normed[j] + parts[j]
            high, low = split(normed[j])
            zh[start : start + n, lanes] = high
            zl[start : start + n, lanes] = low
    zh[W:WP, :] = jnp.zeros((WP - W, C), bf16)
    zl[W:WP, :] = jnp.zeros((WP - W, C), bf16)
    base_ref[W:ROWS, :] = jnp.zeros((ROWS - W, C), f32)
    modes = dot(th_ref[...], zh[...]) + dot(th_ref[...], zl[...]) + dot(tl_ref[...], zh[...])
    modes_ref[...] = modes.astype(bf16)


def pack_kernel(one_ref, one_bias_ref, two_ref, two_bias_ref, out_ref):
    for i, (w_ref, b_ref) in enumerate(((one_ref, one_bias_ref), (two_ref, two_bias_ref))):
        real, imag = w_ref[0], w_ref[1]
        top = jnp.concatenate([real, imag], axis=1)
        bottom = jnp.concatenate([-imag, real], axis=1)
        bias = jnp.concatenate([b_ref[0:1], b_ref[1:2]], axis=1)
        high = bias.astype(bf16).astype(f32)
        rows = lax.broadcasted_iota(jnp.int32, (16, 2 * BS), 0)
        tail = jnp.where(rows == 0, high, jnp.where(rows == 1, bias - high, 0.0))
        out_ref[i] = jnp.concatenate([top, bottom, tail], axis=0).astype(bf16)


def mode_kernel(own_ref, x_ref, fh_ref, fl_ref, gh_ref, gl_ref, *refs):
    w_refs, out_ref, w_all, zh, zl = refs[:NB], refs[NB], refs[NB + 1], refs[NB + 2], refs[NB + 3]
    for slot in range(NB):
        w_all[slot] = w_refs[slot][...]
    own = own_ref[0]
    x = x_ref[...]
    y = dot(fh_ref[...], x) + dot(fl_ref[...], x)

    def layer(values, slot, i):
        high, low = split(values)
        weight = w_all[slot, i, 0 : 2 * BS, :]
        bias = w_all[slot, i, 2 * BS : 2 * BS + 16, :].astype(f32)
        return dot(high, weight) + dot(low, weight) + (bias[0:1] + bias[1:2])

    outs = []
    for b in range(NB):
        slot = jnp.bitwise_xor(own, b)
        lanes = slice(BS * b, BS * b + BS)
        values = jnp.concatenate([y[:H, lanes], y[H:, lanes]], axis=1)
        first = jnp.maximum(layer(values, slot, 0), 0.0)
        second = layer(first, slot, 1)
        outs.append(second - jnp.clip(second, -shrink_level, shrink_level))
    for part in range(2):
        joined = jnp.concatenate([o[:, BS * part : BS * part + BS] for o in outs], axis=1)
        high, low = split(joined)
        zh[H * part : H * part + H, :] = high
        zl[H * part : H * part + H, :] = low
    back = dot(gh_ref[...], zh[...]) + dot(gh_ref[...], zl[...]) + dot(gl_ref[...], zh[...])
    out_ref[...] = back.astype(bf16)


def back_kernel(x_ref, th_ref, tl_ref, base_ref, gain_ref, shift_ref, bias_ref, sum_ref, norm_ref):
    gain = gain_ref[...]
    shift = shift_ref[...]
    bias = bias_ref[...]
    x = x_ref[...]
    for t in range(3):
        rows = slice(TILE * t, TILE * t + TILE)
        total = dot(th_ref[rows, :], x) + dot(tl_ref[rows, :], x) + base_ref[rows, :]
        parts = [total[:, 128 * j : 128 * j + 128] for j in range(6)]
        normed = row_norm(parts, gain, shift)
        norm_ref[rows, :] = jnp.concatenate(normed, axis=1).astype(bf16)
        for j in range(6):
            sum_ref[rows, 128 * j : 128 * j + 128] = parts[j] + bias[j : j + 1, :]


def gelu(x):
    return 0.5 * x * (1.0 + lax.erf(x * 0.7071067811865476))


def mlp_body(x_ref, acc_ref, w_refs, store):
    def tile(t, carry):
        rows = pl.ds(pl.multiple_of(t * TILE, 16), TILE)
        x = x_ref[rows, :]
        acc = acc_ref[rows, :]
        for pair in ((w_refs[0], w_refs[1]), (w_refs[2], w_refs[3])):
            w1 = jnp.concatenate([w[q, 0:BS, :] for w in pair for q in range(4)], axis=0)
            w2 = jnp.concatenate([w[q, BS : 2 * BS, :] for w in pair for q in range(4)], axis=0)
            bias = jnp.concatenate(
                [w[q, 2 * BS : 2 * BS + 16, :].astype(f32)[0:1, 0:BS] for w in pair for q in range(4)], axis=1
            )
            for c in range(3):
                span = slice(256 * c, 256 * c + 256)
                pre = lax.dot_general(x, w1[span], (((1,), (1,)), ((), ())), preferred_element_type=f32)
                hidden = gelu(pre + bias[:, span]).astype(bf16)
                acc = acc + dot(hidden, w2[span])
        store(t, rows, acc)
        return carry

    lax.fori_loop(0, 3, tile, 0)


def mlp_half(x_ref, acc_ref, w0, w1, w2, w3, out_ref):
    def store(t, rows, acc):
        out_ref[rows, :] = acc

    mlp_body(x_ref, acc_ref, (w0, w1, w2, w3), store)


def mlp_last(x_ref, acc_ref, w0, w1, w2, w3, out_ref, total):
    def store(t, rows, acc):
        total[rows, :] = acc

    mlp_body(x_ref, acc_ref, (w0, w1, w2, w3), store)
    for start in range(0, W, 240):
        n = min(240, W - start)
        for j in range(6):
            out_ref[pl.ds(6 * start + j, n, stride=6), :] = total[start : start + n, 128 * j : 128 * j + 128]


def vmem(n):
    return [pl.BlockSpec(memory_space=pltpu.VMEM)] * n


params = pltpu.CompilerParams(vmem_limit_bytes=56 * 2**20)


def place(index):
    lat, chan = divmod(index, 8)
    zh, rest = divmod(lat, 8)
    y, core = divmod(rest, 2)
    zl, x = divmod(chan, 4)
    return x, y, zh * 2 + zl, core


def index_of(x, y, z, core):
    return ((z // 2 * 4 + y) * 2 + core) * 8 + z % 2 * 4 + x


def moves(step):
    return [(d, index_of(*step(*place(d)))) for d in range(256)]


def block_moves(bits):
    return [(d, d // 8 * 8 + ((d % 8) ^ bits)) for d in range(256)]


def spread(value, axes):
    copies = jnp.broadcast_to(value[None], (8,) + value.shape)
    return lax.all_to_all(copies, axes, split_axis=0, concat_axis=0, tiled=True)


def near_moves(n):
    return moves(lambda x, y, z, c: (x, (y + n) % 4, z, c) if c == 0 else ((x + n) % 4, y, z, c))


def far_moves(n):
    return moves(lambda x, y, z, c: ((x + n) % 4, y, z, c) if c == 0 else (x, (y + n) % 4, z, c))


core_moves = moves(lambda x, y, z, c: (x, y, z, 1 - c))


def per_device(
    fields,
    first_gain,
    first_shift,
    filter_one,
    filter_one_bias,
    filter_two,
    filter_two_bias,
    second_gain,
    second_shift,
    dense_weights,
    dense_bias,
    output_bias,
):
    (lon_h, lon_l), (back_h, back_l) = lon_tables()
    (lat_h, lat_l), (tal_h, tal_l) = lat_tables()
    shape = jax.ShapeDtypeStruct

    bias_rows = jnp.pad(dense_bias.reshape(1, 1, 12), ((0, 0), (0, 1), (0, C - 12)))
    shard = jnp.concatenate([dense_weights, bias_rows], axis=0)
    stacked = spread(shard, ("zh", "zl"))

    packed = pl.pallas_call(
        pack_kernel,
        out_shape=shape((2, 2 * BS + 16, 2 * BS), bf16),
        in_specs=vmem(4),
        out_specs=vmem(1)[0],
        compiler_params=params,
        name="pack",
    )(filter_one[0], filter_one_bias[0], filter_two[0], filter_two_bias[0])
    filters = [packed] + [lax.ppermute(packed, AXES, block_moves(b)) for b in range(1, 8)]

    modes, base = pl.pallas_call(
        lon_kernel,
        out_shape=(shape((2 * KW, C), bf16), shape((ROWS, C), f32)),
        in_specs=vmem(5),
        out_specs=tuple(vmem(2)),
        scratch_shapes=[pltpu.VMEM((WP, C), bf16), pltpu.VMEM((WP, C), bf16)],
        compiler_params=params,
        name="lon",
    )(fields.reshape(6 * W, 128), first_gain.reshape(6, 128), first_shift.reshape(6, 128), lon_h, lon_l)

    rows_in = stacked[:, :12, 0, :].reshape(BS, C)
    rows_out = stacked[:, :12, 1, :].reshape(BS, C)
    bias_row = jnp.pad(stacked[:, 12, 0, :12].reshape(1, BS), ((0, 15), (0, C - BS)))
    block = jnp.concatenate([rows_in, rows_out, bias_row], axis=0)
    near = [block] + [lax.ppermute(block, AXES, near_moves(n)) for n in (1, -1, 2)]

    moved = lax.all_to_all(modes.reshape(256, 2, C), AXES, split_axis=0, concat_axis=0, tiled=True)

    group = jnp.stack(near)
    far = [group] + [lax.ppermute(group, AXES, far_moves(n)) for n in (1, -1, 2)]

    own = lax.axis_index(("zl", "x")).astype(jnp.int32).reshape(1)
    mixed = pl.pallas_call(
        mode_kernel,
        out_shape=shape((2 * H, C), bf16),
        in_specs=[pl.BlockSpec(memory_space=pltpu.SMEM)] + vmem(5 + NB),
        out_specs=vmem(1)[0],
        scratch_shapes=[
            pltpu.VMEM((NB, 2, 2 * BS + 16, 2 * BS), bf16),
            pltpu.VMEM((2 * H, C), bf16),
            pltpu.VMEM((2 * H, C), bf16),
        ],
        compiler_params=params,
        name="mode",
    )(own, moved.reshape(2 * H, C), lat_h, lat_l, tal_h, tal_l, *filters)

    returned = lax.all_to_all(mixed.reshape(256, 2, C), AXES, split_axis=0, concat_axis=0, tiled=True)
    other = [lax.ppermute(g, AXES, core_moves) for g in far]

    summed, normed = pl.pallas_call(
        back_kernel,
        out_shape=(shape((ROWS, C), f32), shape((ROWS, C), bf16)),
        in_specs=vmem(7),
        out_specs=tuple(vmem(2)),
        compiler_params=params,
        name="back",
    )(returned.reshape(2 * KW, C), back_h, back_l, base, second_gain.reshape(6, 128), second_shift.reshape(6, 128), output_bias.reshape(6, 128))

    half = pl.pallas_call(
        mlp_half,
        out_shape=shape((ROWS, C), f32),
        in_specs=vmem(6),
        out_specs=vmem(1)[0],
        compiler_params=params,
        name="mlp_half",
    )(normed, summed, *far)
    out = pl.pallas_call(
        mlp_last,
        out_shape=shape((6 * W, 128), f32),
        in_specs=vmem(6),
        out_specs=vmem(1)[0],
        scratch_shapes=[pltpu.VMEM((ROWS, C), f32)],
        compiler_params=params,
        name="mlp_last",
    )(normed, half, *other)
    return out.reshape(1, W, C)


def solution(mesh):
    fine = Mesh(mesh.devices.reshape(4, 4, 2, 2, 4), AXES)
    chan = AXES[3:]
    placed = (
        P(AXES, None, None),
        P(),
        P(),
        P(chan, None, None, None),
        P(chan, None, None),
        P(chan, None, None, None),
        P(chan, None, None),
        P(),
        P(),
        P(AXES, None, None),
        P(AXES),
        P(),
    )
    return jax.shard_map(
        per_device, mesh=fine, in_specs=placed, out_specs=P(AXES, None, None), check_vma=False
    )
```

```python
import functools

import jax
import jax.numpy as jnp
import numpy as np
from jax import lax
from jax.experimental import pallas as pl
from jax.experimental.pallas import tpu as pltpu
from jax.sharding import Mesh
from jax.sharding import PartitionSpec as P


W = 900
WP = 1024
KW = 256
H = 256
C = 768
BS = 96
NB = 8
TILE = 304
ROWS = 3 * TILE
norm_eps = 1e-05
shrink_level = 0.01
AXES = ("zh", "y", "co", "zl", "x")
bf16 = jnp.bfloat16
f32 = jnp.float32


def split_table(values):
    high = values.astype(np.float32).astype(jnp.bfloat16)
    low = (values - high.astype(np.float64)).astype(np.float32).astype(jnp.bfloat16)
    return high, low


def lon_tables():
    k = np.arange(KW)[:, None]
    w = np.arange(W)[None, :]
    angle = 2 * np.pi * (k * w % W) / W
    forward = np.zeros((KW, 2, WP))
    forward[:, 0, :W] = np.cos(angle)
    forward[:, 1, :W] = -np.sin(angle)
    forward = forward.reshape(2 * KW, WP) * W**-0.5
    factor = np.where(k == 0, 1.0, 2.0)
    backward = np.zeros((ROWS, KW, 2))
    backward[:W, :, 0] = (np.cos(angle) * factor).T
    backward[:W, :, 1] = (-np.sin(angle) * factor).T
    backward = backward.reshape(ROWS, 2 * KW) * W**-0.5
    return split_table(forward), split_table(backward)


def lat_tables():
    m = np.arange(H)[:, None]
    h = np.arange(H)[None, :]
    angle = 2 * np.pi * (m * h % H) / H
    cos, sin = np.cos(angle), np.sin(angle)
    forward = np.zeros((2, H, H, 2))
    forward[0, :, :, 0] = cos
    forward[0, :, :, 1] = sin
    forward[1, :, :, 0] = -sin
    forward[1, :, :, 1] = cos
    forward = forward.reshape(2 * H, 2 * H) * H**-0.5
    return split_table(forward), split_table(forward.T)


def dot(a, b):
    return jnp.dot(a, b, preferred_element_type=f32)


def split(x):
    high = x.astype(bf16)
    return high, (x - high.astype(f32)).astype(bf16)


def row_norm(parts, gain, shift):
    count = len(parts) * 128
    mean = jnp.sum(functools.reduce(jnp.add, parts), axis=-1, keepdims=True) / count
    centered = [p - mean for p in parts]
    square = functools.reduce(jnp.add, [c * c for c in centered])
    scale = lax.rsqrt(jnp.sum(square, axis=-1, keepdims=True) / count + norm_eps)
    return [
        c * scale * gain[j : j + 1, :] + shift[j : j + 1, :]
        for j, c in enumerate(centered)
    ]


def start(copies):
    for copy in copies:
        copy.start()


def lon_kernel(x_hbm, gain_ref, shift_ref, th_hbm, tl_hbm, modes_ref, base_hbm, x_ref, th, tl, base, zh, zl, sem, out_sem):
    spans = [(r, min(240, W - r)) for r in range(0, W, 240)]
    loads = [
        pltpu.make_async_copy(x_hbm.at[pl.ds(6 * r, 6 * n)], x_ref.at[pl.ds(6 * r, 6 * n)], sem.at[i])
        for i, (r, n) in enumerate(spans)
    ]
    tables = [pltpu.make_async_copy(th_hbm, th, sem.at[4]), pltpu.make_async_copy(tl_hbm, tl, sem.at[5])]
    start(loads + tables)
    gain = gain_ref[...]
    shift = shift_ref[...]
    stores = []
    for i, (r, n) in enumerate(spans):
        loads[i].wait()
        parts = [x_ref[pl.ds(6 * r + j, n, stride=6), :] for j in range(6)]
        normed = row_norm(parts, gain, shift)
        for j in range(6):
            lanes = slice(128 * j, 128 * j + 128)
            base[r : r + n, lanes] = normed[j] + parts[j]
            high, low = split(normed[j])
            zh[r : r + n, lanes] = high
            zl[r : r + n, lanes] = low
        if r + n == W:
            base[W:ROWS, :] = jnp.zeros((ROWS - W, C), f32)
            n = ROWS - r
        stores.append(pltpu.make_async_copy(base.at[pl.ds(r, n)], base_hbm.at[pl.ds(r, n)], out_sem.at[i]))
        stores[-1].start()
    zh[W:WP, :] = jnp.zeros((WP - W, C), bf16)
    zl[W:WP, :] = jnp.zeros((WP - W, C), bf16)
    tables[0].wait()
    modes = dot(th[...], zh[...]) + dot(th[...], zl[...])
    tables[1].wait()
    modes = modes + dot(tl[...], zh[...])
    modes_ref[...] = modes.astype(bf16).reshape(KW, 2, C)
    for copy in stores:
        copy.wait()


def pack_kernel(one_ref, one_bias_ref, two_ref, two_bias_ref, out_ref):
    for i, (w_ref, b_ref) in enumerate(((one_ref, one_bias_ref), (two_ref, two_bias_ref))):
        top = jnp.concatenate([w_ref[0], w_ref[1]], axis=1)
        bias = jnp.concatenate([b_ref[0:1], b_ref[1:2]], axis=1)
        high = bias.astype(bf16).astype(f32)
        rows = lax.broadcasted_iota(jnp.int32, (16, 2 * BS), 0)
        tail = jnp.where(rows == 0, high, jnp.where(rows == 1, bias - high, 0.0))
        out_ref[i] = jnp.concatenate([top, tail], axis=0).astype(bf16)


def mode_kernel(own_ref, x_hbm, fh_hbm, fl_hbm, gh_hbm, gl_hbm, w0, w1, w2, w3, out_ref, x_ref, fh, fl, gh, gl, w_all, zh, zl, sem):
    pairs = [(x_hbm, x_ref), (fh_hbm, fh), (fl_hbm, fl)] + [(w, w_all.at[d]) for d, w in enumerate((w0, w1, w2, w3))]
    pairs += [(gh_hbm, gh), (gl_hbm, gl)]
    copies = [pltpu.make_async_copy(source, target, sem.at[i]) for i, (source, target) in enumerate(pairs)]
    start(copies)
    own = own_ref[0]
    copies[0].wait()
    copies[1].wait()
    x = x_ref[...].reshape(2 * H, C)
    y = dot(fh[...], x)
    copies[2].wait()
    y = y + dot(fl[...], x)
    for copy in copies[3:7]:
        copy.wait()

    def layer(values, slot, i):
        high, low = split(values)
        packed = w_all[jnp.bitwise_and(slot, 3), lax.shift_right_logical(slot, 2), i]
        top = packed[0:BS]
        bottom = jnp.concatenate([-top[:, BS:], top[:, :BS]], axis=1)
        weight = jnp.concatenate([top, bottom], axis=0)
        bias = packed[BS : BS + 16].astype(f32)
        return dot(high, weight) + dot(low, weight) + (bias[0:1] + bias[1:2])

    outs = []
    for b in range(NB):
        slot = jnp.bitwise_xor(own, b)
        lanes = slice(BS * b, BS * b + BS)
        values = jnp.concatenate([y[:H, lanes], y[H:, lanes]], axis=1)
        first = jnp.maximum(layer(values, slot, 0), 0.0)
        second = layer(first, slot, 1)
        outs.append(second - jnp.clip(second, -shrink_level, shrink_level))
    for part in range(2):
        joined = jnp.concatenate([o[:, BS * part : BS * part + BS] for o in outs], axis=1)
        high, low = split(joined)
        zh[H * part : H * part + H, :] = high
        zl[H * part : H * part + H, :] = low
    copies[7].wait()
    back = dot(gh[...], zh[...]) + dot(gh[...], zl[...])
    copies[8].wait()
    back = back + dot(gl[...], zh[...])
    out_ref[...] = back.astype(bf16).reshape(H, 2, C)


def gelu(x):
    return 0.5 * x * (1.0 + lax.erf(x * 0.7071067811865476))


def tail_kernel(x_hbm, th_hbm, tl_hbm, base_hbm, gain_ref, shift_ref, bias_ref, *refs):
    w_hbm, out_hbm = refs[:8], refs[8]
    x_ref, th, tl, base, weights, normed, result, sem, w_sem, out_sem = refs[9:]
    pairs = [(x_hbm, x_ref), (th_hbm, th), (tl_hbm, tl), (base_hbm, base)]
    copies = [pltpu.make_async_copy(source, target, sem.at[i]) for i, (source, target) in enumerate(pairs)]
    w_copies = [pltpu.make_async_copy(w, weights.at[pl.ds(4 * i, 4)], w_sem.at[i]) for i, w in enumerate(w_hbm)]
    start(copies + w_copies)
    gain = gain_ref[...]
    shift = shift_ref[...]
    out_bias = bias_ref[...]
    for copy in copies:
        copy.wait()
    x = x_ref[...].reshape(2 * KW, C)
    for t in range(3):
        rows = slice(TILE * t, TILE * t + TILE)
        total = dot(th[rows, :], x) + dot(tl[rows, :], x) + base[rows, :]
        parts = [total[:, 128 * j : 128 * j + 128] for j in range(6)]
        normed[rows, :] = jnp.concatenate(row_norm(parts, gain, shift), axis=1).astype(bf16)
        for j in range(6):
            base[rows, 128 * j : 128 * j + 128] = parts[j] + out_bias[j : j + 1, :]
    for copy in w_copies:
        copy.wait()

    def out_copy(t, n):
        span = pl.ds(6 * TILE * t, 6 * n)
        return pltpu.make_async_copy(result.at[span], out_hbm.at[span], out_sem.at[t])

    def tile(t, carry):
        rows = pl.ds(pl.multiple_of(t * TILE, 16), TILE)
        tokens = normed[rows, :]
        acc = base[rows, :]
        for first in range(0, 32, 8):
            w1 = jnp.concatenate([weights[q, 0:BS, :] for q in range(first, first + 8)], axis=0)
            w2 = jnp.concatenate([weights[q, BS : 2 * BS, :] for q in range(first, first + 8)], axis=0)
            bias = jnp.concatenate(
                [weights[q, 2 * BS : 2 * BS + 16, :].astype(f32)[0:1, 0:BS] for q in range(first, first + 8)], axis=1
            )
            for c in range(3):
                span = slice(256 * c, 256 * c + 256)
                pre = lax.dot_general(tokens, w1[span], (((1,), (1,)), ((), ())), preferred_element_type=f32)
                hidden = gelu(pre + bias[:, span]).astype(bf16)
                acc = acc + dot(hidden, w2[span])
        for j in range(6):
            result[pl.ds(6 * TILE * t + j, TILE, stride=6), :] = acc[:, 128 * j : 128 * j + 128]

        @pl.when(t < 2)
        def _():
            out_copy(t, TILE).start()

        return carry

    lax.fori_loop(0, 3, tile, 0)
    last = out_copy(2, W - 2 * TILE)
    last.start()
    out_copy(0, TILE).wait()
    out_copy(1, TILE).wait()
    last.wait()


def vmem(n):
    return [pl.BlockSpec(memory_space=pltpu.VMEM)] * n


def anywhere(n):
    return [pl.BlockSpec(memory_space=pl.ANY)] * n


params = pltpu.CompilerParams(vmem_limit_bytes=56 * 2**20)


def place(index):
    lat, chan = divmod(index, 8)
    zh, rest = divmod(lat, 8)
    y, core = divmod(rest, 2)
    zl, x = divmod(chan, 4)
    return x, y, zh * 2 + zl, core


def index_of(x, y, z, core):
    return ((z // 2 * 4 + y) * 2 + core) * 8 + z % 2 * 4 + x


def moves(step):
    return [(d, index_of(*step(*place(d)))) for d in range(256)]


def block_moves(bits):
    return [(d, d ^ bits) for d in range(256)]


def spread(value, axes):
    copies = jnp.broadcast_to(value[None], (8,) + value.shape)
    return lax.all_to_all(copies, axes, split_axis=0, concat_axis=0, tiled=True)


def near_moves(n):
    return moves(lambda x, y, z, c: (x, (y + n) % 4, z, c) if c == 0 else ((x + n) % 4, y, z, c))


def far_moves(n):
    return moves(lambda x, y, z, c: ((x + n) % 4, y, z, c) if c == 0 else (x, (y + n) % 4, z, c))


core_moves = moves(lambda x, y, z, c: (x, y, z, 1 - c))


def per_device(
    fields,
    first_gain,
    first_shift,
    filter_one,
    filter_one_bias,
    filter_two,
    filter_two_bias,
    second_gain,
    second_shift,
    dense_weights,
    dense_bias,
    output_bias,
):
    (lon_h, lon_l), (back_h, back_l) = lon_tables()
    (lat_h, lat_l), (tal_h, tal_l) = lat_tables()
    shape = jax.ShapeDtypeStruct

    bias_rows = jnp.pad(dense_bias.reshape(1, 1, 12), ((0, 0), (0, 1), (0, C - 12)))
    shard = jnp.concatenate([dense_weights, bias_rows], axis=0)
    stacked = spread(shard, ("zh", "zl"))

    packed = pl.pallas_call(
        pack_kernel,
        out_shape=shape((2, BS + 16, 2 * BS), bf16),
        in_specs=vmem(4),
        out_specs=vmem(1)[0],
        compiler_params=params,
        name="pack",
    )(filter_one[0], filter_one_bias[0], filter_two[0], filter_two_bias[0])
    partner = lax.ppermute(packed, AXES, block_moves(4))

    modes, base = pl.pallas_call(
        lon_kernel,
        out_shape=(shape((KW, 2, C), bf16), shape((ROWS, C), f32)),
        in_specs=anywhere(1) + vmem(2) + anywhere(2),
        out_specs=(vmem(1)[0], anywhere(1)[0]),
        scratch_shapes=[
            pltpu.VMEM((6 * W, 128), f32),
            pltpu.VMEM((2 * KW, WP), bf16),
            pltpu.VMEM((2 * KW, WP), bf16),
            pltpu.VMEM((ROWS, C), f32),
            pltpu.VMEM((WP, C), bf16),
            pltpu.VMEM((WP, C), bf16),
            pltpu.SemaphoreType.DMA((6,)),
            pltpu.SemaphoreType.DMA((4,)),
        ],
        compiler_params=params,
        name="lon",
    )(fields.reshape(6 * W, 128), first_gain.reshape(6, 128), first_shift.reshape(6, 128), lon_h, lon_l)

    pair = jnp.stack([packed, partner])
    filters = [pair] + [lax.ppermute(pair, AXES, block_moves(b)) for b in range(1, 4)]

    rows_in = stacked[:, :12, 0, :].reshape(BS, C)
    rows_out = stacked[:, :12, 1, :].reshape(BS, C)
    bias_row = jnp.pad(stacked[:, 12, 0, :12].reshape(1, BS), ((0, 15), (0, C - BS)))
    block = jnp.concatenate([rows_in, rows_out, bias_row], axis=0)
    near = [block] + [lax.ppermute(block, AXES, near_moves(n)) for n in (1, -1, 2)]

    moved = lax.all_to_all(modes, AXES, split_axis=0, concat_axis=0, tiled=True)

    group = jnp.stack(near)
    far = [group] + [lax.ppermute(group, AXES, far_moves(n)) for n in (1, -1, 2)]

    own = lax.axis_index(("zl", "x")).astype(jnp.int32).reshape(1)
    mixed = pl.pallas_call(
        mode_kernel,
        out_shape=shape((H, 2, C), bf16),
        in_specs=[pl.BlockSpec(memory_space=pltpu.SMEM)] + anywhere(9),
        out_specs=vmem(1)[0],
        scratch_shapes=[pltpu.VMEM((H, 2, C), bf16)]
        + [pltpu.VMEM((2 * H, 2 * H), bf16)] * 4
        + [
            pltpu.VMEM((4, 2, 2, BS + 16, 2 * BS), bf16),
            pltpu.VMEM((2 * H, C), bf16),
            pltpu.VMEM((2 * H, C), bf16),
            pltpu.SemaphoreType.DMA((9,)),
        ],
        compiler_params=params,
        name="mode",
    )(own, moved, lat_h, lat_l, tal_h, tal_l, *filters)

    returned = lax.all_to_all(mixed, AXES, split_axis=0, concat_axis=0, tiled=True)
    other = [lax.ppermute(g, AXES, core_moves) for g in far]

    out = pl.pallas_call(
        tail_kernel,
        out_shape=shape((6 * W, 128), f32),
        in_specs=anywhere(4) + vmem(3) + anywhere(8),
        out_specs=anywhere(1)[0],
        scratch_shapes=[
            pltpu.VMEM((KW, 2, C), bf16),
            pltpu.VMEM((ROWS, 2 * KW), bf16),
            pltpu.VMEM((ROWS, 2 * KW), bf16),
            pltpu.VMEM((ROWS, C), f32),
            pltpu.VMEM((32, 2 * BS + 16, C), bf16),
            pltpu.VMEM((ROWS, C), bf16),
            pltpu.VMEM((6 * ROWS, 128), f32),
            pltpu.SemaphoreType.DMA((4,)),
            pltpu.SemaphoreType.DMA((8,)),
            pltpu.SemaphoreType.DMA((3,)),
        ],
        compiler_params=params,
        name="tail",
    )(
        returned,
        back_h,
        back_l,
        base,
        second_gain.reshape(6, 128),
        second_shift.reshape(6, 128),
        output_bias.reshape(6, 128),
        *far,
        *other,
    )
    return out.reshape(1, W, C)


def solution(mesh):
    fine = Mesh(mesh.devices.reshape(4, 4, 2, 2, 4), AXES)
    chan = AXES[3:]
    placed = (
        P(AXES, None, None),
        P(),
        P(),
        P(chan, None, None, None),
        P(chan, None, None),
        P(chan, None, None, None),
        P(chan, None, None),
        P(),
        P(),
        P(AXES, None, None),
        P(AXES),
        P(),
    )
    return jax.shard_map(
        per_device, mesh=fine, in_specs=placed, out_specs=P(AXES, None, None), check_vma=False
    )
```

```python
import functools

import jax
import jax.numpy as jnp
import numpy as np
from jax import lax
from jax.experimental import pallas as pl
from jax.experimental.pallas import tpu as pltpu
from jax.sharding import Mesh
from jax.sharding import PartitionSpec as P


W = 900
HALF = 450
WP = 512
STEP = 149
PART = 152
KW = 256
H = 256
C = 768
BS = 96
NB = 8
TILE = 2 * PART
ROWS = 3 * TILE
norm_eps = 1e-05
shrink_level = 0.01
AXES = ("zh", "y", "co", "zl", "x")
bf16 = jnp.bfloat16
f32 = jnp.float32


def split_table(values):
    high = values.astype(np.float32).astype(jnp.bfloat16)
    low = (values - high.astype(np.float64)).astype(np.float32).astype(jnp.bfloat16)
    return high, low


def lon_tables():
    k = np.arange(KW).reshape(KW // 2, 2).T
    w = np.arange(HALF)
    angle = 2 * np.pi * (k[:, :, None] * w % W) / W
    forward = np.zeros((2, KW // 2, 2, WP))
    forward[:, :, 0, :HALF] = np.cos(angle)
    forward[:, :, 1, :HALF] = -np.sin(angle)
    forward = forward.reshape(2, KW, WP) * W**-0.5
    factor = np.where(k == 0, 1.0, 2.0)[:, :, None]
    waves = np.stack([np.cos(angle) * factor, -np.sin(angle) * factor], axis=2).reshape(2, KW, HALF) * W**-0.5
    backward = np.stack([waves[:, :, STEP * t : STEP * t + PART].transpose(0, 2, 1) for t in range(3)])
    return split_table(forward), split_table(backward)


def lat_tables():
    m = np.arange(H).reshape(H // 2, 2).T.reshape(H)[:, None]
    h = np.arange(H)[None, :]
    angle = 2 * np.pi * (m * h % H) / H
    cos, sin = np.cos(angle), np.sin(angle)
    forward = np.zeros((2, H, H, 2))
    forward[0, :, :, 0] = cos
    forward[0, :, :, 1] = sin
    forward[1, :, :, 0] = -sin
    forward[1, :, :, 1] = cos
    forward = forward * H**-0.5
    parity = forward.reshape(2, 2, H // 2, H, 2)[:, :, :, : H // 2, :]
    backward = parity.transpose(1, 3, 4, 0, 2).reshape(2, H, H)
    return split_table(forward.reshape(2 * H, 2 * H)), split_table(backward)


def dot(a, b):
    return jnp.dot(a, b, preferred_element_type=f32)


def split(x):
    high = x.astype(bf16)
    return high, (x - high.astype(f32)).astype(bf16)


def row_norm(parts, gain, shift):
    count = len(parts) * 128
    mean = jnp.sum(functools.reduce(jnp.add, parts), axis=-1, keepdims=True) / count
    centered = [p - mean for p in parts]
    square = functools.reduce(jnp.add, [c * c for c in centered])
    scale = lax.rsqrt(jnp.sum(square, axis=-1, keepdims=True) / count + norm_eps)
    return [
        c * scale * gain[j : j + 1, :] + shift[j : j + 1, :]
        for j, c in enumerate(centered)
    ]


def start(copies):
    for copy in copies:
        copy.start()


def pack_filters(refs, out_ref):
    for i, (w_ref, b_ref) in enumerate((refs[:2], refs[2:])):
        top = jnp.concatenate([w_ref[0], w_ref[1]], axis=1)
        bias = jnp.concatenate([b_ref[0:1], b_ref[1:2]], axis=1)
        high = bias.astype(bf16).astype(f32)
        rows = lax.broadcasted_iota(jnp.int32, (16, 2 * BS), 0)
        tail = jnp.where(rows == 0, high, jnp.where(rows == 1, bias - high, 0.0))
        out_ref[i] = jnp.concatenate([top, tail], axis=0).astype(bf16)


def lon_kernel(x_hbm, gain_ref, shift_ref, th_hbm, tl_hbm, f0, f1, f2, f3, *refs):
    modes_ref, base_hbm, pack_ref, x_ref, th, tl, base, high, low, sem, out_sem = refs
    cuts = (0, 960, 1920, 2696, 3664, 4624, 5400)
    loads = [
        pltpu.make_async_copy(x_hbm.at[pl.ds(p, q - p)], x_ref.at[pl.ds(p, q - p)], sem.at[i])
        for i, (p, q) in enumerate(zip(cuts[:-1], cuts[1:]))
    ]
    tables = [pltpu.make_async_copy(th_hbm, th, sem.at[6]), pltpu.make_async_copy(tl_hbm, tl, sem.at[7])]
    start([loads[i] for i in (0, 3, 1, 4, 2, 5)] + tables)
    pack_filters((f0, f1, f2, f3), pack_ref)
    gain = gain_ref[...]
    shift = shift_ref[...]
    for parity in range(2):
        high[parity, 448:WP, :] = jnp.zeros((WP - 448, C), bf16)
        low[parity, 448:WP, :] = jnp.zeros((WP - 448, C), bf16)
    for i, (r, n) in enumerate(((0, 160), (160, 160), (320, 130))):
        loads[i].wait()
        loads[i + 3].wait()
        pairs = []
        for first in (r, HALF + r):
            parts = [x_ref[pl.ds(6 * first + j, n, stride=6), :] for j in range(6)]
            normed = row_norm(parts, gain, shift)
            for j in range(6):
                base[pl.ds(6 * first + j, n, stride=6), :] = normed[j] + parts[j]
            pairs.append(normed)
        for j in range(6):
            lanes = slice(128 * j, 128 * j + 128)
            for parity, value in enumerate((pairs[0][j] + pairs[1][j], pairs[0][j] - pairs[1][j])):
                high[parity, r : r + n, lanes], low[parity, r : r + n, lanes] = split(value)
    store = pltpu.make_async_copy(base, base_hbm, out_sem)
    store.start()
    tables[0].wait()
    tables[1].wait()
    for parity in range(2):
        modes = dot(th[parity], high[parity]) + dot(th[parity], low[parity]) + dot(tl[parity], high[parity])
        modes_ref[128 * parity : 128 * parity + 128] = modes.astype(bf16).reshape(KW // 2, 2, C)
    store.wait()


def mode_kernel(own_ref, x_hbm, fh_hbm, fl_hbm, gh_hbm, gl_hbm, w0, w1, w2, w3, out_ref, x_ref, fh, fl, gh, gl, w_all, zh, zl, sem):
    pairs = [(x_hbm, x_ref), (fh_hbm, fh), (fl_hbm, fl)] + [(w, w_all.at[d]) for d, w in enumerate((w0, w1, w2, w3))]
    pairs += [(gh_hbm, gh), (gl_hbm, gl)]
    copies = [pltpu.make_async_copy(source, target, sem.at[i]) for i, (source, target) in enumerate(pairs)]
    start(copies)
    own = own_ref[0]
    copies[0].wait()
    copies[1].wait()
    x = x_ref[...].reshape(2 * H, C)
    y = dot(fh[...], x)
    copies[2].wait()
    y = y + dot(fl[...], x)
    for copy in copies[3:7]:
        copy.wait()

    def layer(values, slot, i):
        high, low = split(values)
        packed = w_all[jnp.bitwise_and(slot, 3), lax.shift_right_logical(slot, 2), i]
        top = packed[0:BS]
        bottom = jnp.concatenate([-top[:, BS:], top[:, :BS]], axis=1)
        weight = jnp.concatenate([top, bottom], axis=0)
        bias = packed[BS : BS + 16].astype(f32)
        return dot(high, weight) + dot(low, weight) + (bias[0:1] + bias[1:2])

    outs = []
    for b in range(NB):
        slot = jnp.bitwise_xor(own, b)
        lanes = slice(BS * b, BS * b + BS)
        values = jnp.concatenate([y[:H, lanes], y[H:, lanes]], axis=1)
        first = jnp.maximum(layer(values, slot, 0), 0.0)
        second = layer(first, slot, 1)
        outs.append(second - jnp.clip(second, -shrink_level, shrink_level))
    for part in range(2):
        joined = jnp.concatenate([o[:, BS * part : BS * part + BS] for o in outs], axis=1)
        high, low = split(joined)
        for parity in range(2):
            rows = slice(H // 2 * parity, H // 2 * parity + H // 2)
            spot = slice(H // 2 * part, H // 2 * part + H // 2)
            zh[parity, spot, :] = high[rows]
            zl[parity, spot, :] = low[rows]
    copies[7].wait()
    copies[8].wait()
    even, odd = [dot(gh[p], zh[p]) + dot(gh[p], zl[p]) + dot(gl[p], zh[p]) for p in range(2)]
    out_ref[0 : H // 2] = (even + odd).astype(bf16).reshape(H // 2, 2, C)
    out_ref[H // 2 : H] = (even - odd).astype(bf16).reshape(H // 2, 2, C)


def gelu(x):
    return 0.5 * x * (1.0 + lax.erf(x * 0.7071067811865476))


def tail_kernel(x_hbm, th_hbm, tl_hbm, base_hbm, gain_ref, shift_ref, bias_ref, *refs):
    w_hbm, out_hbm = refs[:10], refs[10]
    x_ref, th, tl, base, weights, normed, summed, result, sem, w_sem, out_sem = refs[11:]
    pairs = [(x_hbm, x_ref), (th_hbm, th), (tl_hbm, tl), (base_hbm, base)]
    copies = [pltpu.make_async_copy(source, target, sem.at[i]) for i, (source, target) in enumerate(pairs)]
    w_copies = []
    spot = 0
    for i, w in enumerate(w_hbm):
        w_copies.append(pltpu.make_async_copy(w, weights.at[pl.ds(spot, w.shape[0])], w_sem.at[i]))
        spot += w.shape[0]
    start(copies + w_copies)
    gain = gain_ref[...]
    shift = shift_ref[...]
    out_bias = bias_ref[...]
    for copy in copies:
        copy.wait()
    x = x_ref[...].reshape(2 * KW, C)
    for t in range(3):
        even, odd = [dot(th[t, p], x[KW * p : KW * p + KW]) + dot(tl[t, p], x[KW * p : KW * p + KW]) for p in range(2)]
        parts = []
        for j in range(6):
            lanes = slice(128 * j, 128 * j + 128)
            near = base[pl.ds(6 * STEP * t + j, PART, stride=6), :]
            far = base[pl.ds(6 * (STEP * t + HALF) + j, PART, stride=6), :]
            parts.append(
                jnp.concatenate([even[:, lanes] + odd[:, lanes] + near, even[:, lanes] - odd[:, lanes] + far], axis=0)
            )
        rows = slice(TILE * t, TILE * t + TILE)
        normed[rows, :] = jnp.concatenate(row_norm(parts, gain, shift), axis=1).astype(bf16)
        for j in range(6):
            summed[rows, 128 * j : 128 * j + 128] = parts[j] + out_bias[j : j + 1, :]
    for copy in w_copies:
        copy.wait()

    def out_copy(i, first, last):
        span = pl.ds(first, last - first)
        return pltpu.make_async_copy(result.at[span], out_hbm.at[span], out_sem.at[i])

    outs = [out_copy(i, *c) for i, c in enumerate(((0, 1784), (2704, 4488), (1784, 2704), (4488, 5400)))]

    def tile(t, carry):
        rows = pl.ds(pl.multiple_of(t * TILE, 16), TILE)
        tokens = normed[rows, :]
        acc = summed[rows, :]
        for first in range(0, 32, 8):
            w1 = jnp.concatenate([weights[q, 0:BS, :] for q in range(first, first + 8)], axis=0)
            w2 = jnp.concatenate([weights[q, BS : 2 * BS, :] for q in range(first, first + 8)], axis=0)
            bias = jnp.concatenate(
                [weights[q, 2 * BS : 2 * BS + 16, :].astype(f32)[0:1, 0:BS] for q in range(first, first + 8)], axis=1
            )
            for c in range(3):
                span = slice(256 * c, 256 * c + 256)
                pre = lax.dot_general(tokens, w1[span], (((1,), (1,)), ((), ())), preferred_element_type=f32)
                hidden = gelu(pre + bias[:, span]).astype(bf16)
                acc = acc + dot(hidden, w2[span])
        for j in range(6):
            lanes = slice(128 * j, 128 * j + 128)
            result[pl.ds(6 * STEP * t + j, PART, stride=6), :] = acc[:PART, lanes]
            result[pl.ds(6 * STEP * t + 6 * HALF + j, PART, stride=6), :] = acc[PART:, lanes]

        @pl.when(t == 1)
        def _():
            outs[0].start()
            outs[1].start()

        return carry

    lax.fori_loop(0, 3, tile, 0)
    outs[2].start()
    outs[3].start()
    for copy in outs:
        copy.wait()


def vmem(n):
    return [pl.BlockSpec(memory_space=pltpu.VMEM)] * n


def anywhere(n):
    return [pl.BlockSpec(memory_space=pl.ANY)] * n


params = pltpu.CompilerParams(vmem_limit_bytes=56 * 2**20)


def place(index):
    lat, chan = divmod(index, 8)
    zh, rest = divmod(lat, 8)
    y, core = divmod(rest, 2)
    zl, x = divmod(chan, 4)
    return x, y, zh * 2 + zl, core


def index_of(x, y, z, core):
    return ((z // 2 * 4 + y) * 2 + core) * 8 + z % 2 * 4 + x


def moves(step):
    return [(d, index_of(*step(*place(d)))) for d in range(256)]


def block_moves(bits):
    return [(d, d ^ bits) for d in range(256)]


def z_moves(bits):
    return moves(lambda x, y, z, c: (x, y, z ^ bits, c))


def near_moves(n):
    return moves(lambda x, y, z, c: (x, (y + n) % 4, z, c) if c == 0 else ((x + n) % 4, y, z, c))


def far_moves(n):
    return moves(lambda x, y, z, c: ((x + n) % 4, y, z, c) if c == 0 else (x, (y + n) % 4, z, c))


core_moves = moves(lambda x, y, z, c: (x, y, z, 1 - c))


def per_device(
    fields,
    first_gain,
    first_shift,
    filter_one,
    filter_one_bias,
    filter_two,
    filter_two_bias,
    second_gain,
    second_shift,
    dense_weights,
    dense_bias,
    output_bias,
):
    (lon_h, lon_l), (back_h, back_l) = lon_tables()
    (lat_h, lat_l), (tal_h, tal_l) = lat_tables()
    shape = jax.ShapeDtypeStruct

    bias_rows = jnp.pad(dense_bias.reshape(1, 1, 12), ((0, 0), (0, 1), (0, C - 12)))
    shard = jnp.concatenate([dense_weights, bias_rows], axis=0)
    one = lax.ppermute(shard, AXES, z_moves(1))

    modes, base, packed = pl.pallas_call(
        lon_kernel,
        out_shape=(shape((KW, 2, C), bf16), shape((6 * W, 128), f32), shape((2, BS + 16, 2 * BS), bf16)),
        in_specs=anywhere(1) + vmem(2) + anywhere(2) + vmem(4),
        out_specs=(vmem(1)[0], anywhere(1)[0], vmem(1)[0]),
        scratch_shapes=[
            pltpu.VMEM((6 * W, 128), f32),
            pltpu.VMEM((2, KW, WP), bf16),
            pltpu.VMEM((2, KW, WP), bf16),
            pltpu.VMEM((6 * W, 128), f32),
            pltpu.VMEM((2, WP, C), bf16),
            pltpu.VMEM((2, WP, C), bf16),
            pltpu.SemaphoreType.DMA((8,)),
            pltpu.SemaphoreType.DMA,
        ],
        compiler_params=params,
        name="lon",
    )(
        fields.reshape(6 * W, 128),
        first_gain.reshape(6, 128),
        first_shift.reshape(6, 128),
        lon_h,
        lon_l,
        filter_one[0],
        filter_one_bias[0],
        filter_two[0],
        filter_two_bias[0],
    )

    two = jnp.concatenate([shard, one], axis=0)
    four = jnp.concatenate([two, lax.ppermute(two, AXES, z_moves(2))], axis=0)
    eight = jnp.concatenate([four, lax.ppermute(four, AXES, z_moves(4))], axis=0)
    stacked = eight.reshape(8, 13, 2, C)
    partner = lax.ppermute(packed, AXES, block_moves(4))
    pair = jnp.stack([packed, partner])
    filters = [pair] + [lax.ppermute(pair, AXES, block_moves(b)) for b in range(1, 4)]

    rows_in = stacked[:, :12, 0, :].reshape(BS, C)
    rows_out = stacked[:, :12, 1, :].reshape(BS, C)
    bias_row = jnp.pad(stacked[:, 12, 0, :12].reshape(1, BS), ((0, 15), (0, C - BS)))
    block = jnp.concatenate([rows_in, rows_out, bias_row], axis=0)
    near = [block] + [lax.ppermute(block, AXES, near_moves(n)) for n in (1, -1, 2)]

    moved = lax.all_to_all(modes, AXES, split_axis=0, concat_axis=0, tiled=True)

    group = jnp.stack(near)
    left = lax.ppermute(group, AXES, far_moves(1))
    right = lax.ppermute(group, AXES, far_moves(-1))
    across = [lax.ppermute(left[:2], AXES, far_moves(1)), lax.ppermute(right[2:], AXES, far_moves(-1))]
    far = [group, left, right] + across

    own = lax.axis_index(("zl", "x")).astype(jnp.int32).reshape(1)
    mode_call = pl.pallas_call(
        mode_kernel,
        out_shape=shape((H, 2, C), bf16),
        in_specs=[pl.BlockSpec(memory_space=pltpu.SMEM)] + anywhere(9),
        out_specs=vmem(1)[0],
        scratch_shapes=[pltpu.VMEM((H, 2, C), bf16)]
        + [pltpu.VMEM((2 * H, 2 * H), bf16)] * 2
        + [pltpu.VMEM((2, H, H), bf16)] * 2
        + [
            pltpu.VMEM((4, 2, 2, BS + 16, 2 * BS), bf16),
            pltpu.VMEM((2, H, C), bf16),
            pltpu.VMEM((2, H, C), bf16),
            pltpu.SemaphoreType.DMA((9,)),
        ],
        compiler_params=params,
        name="mode",
    )
    mixed = mode_call(own, moved, lat_h, lat_l, tal_h, tal_l, *filters)

    returned = lax.all_to_all(mixed, AXES, split_axis=0, concat_axis=0, tiled=True)
    other = [lax.ppermute(g, AXES, core_moves) for g in far]

    out = pl.pallas_call(
        tail_kernel,
        out_shape=shape((6 * W, 128), f32),
        in_specs=anywhere(4) + vmem(3) + anywhere(10),
        out_specs=anywhere(1)[0],
        scratch_shapes=[
            pltpu.VMEM((KW, 2, C), bf16),
            pltpu.VMEM((3, 2, PART, KW), bf16),
            pltpu.VMEM((3, 2, PART, KW), bf16),
            pltpu.VMEM((6 * W, 128), f32),
            pltpu.VMEM((32, 2 * BS + 16, C), bf16),
            pltpu.VMEM((ROWS, C), bf16),
            pltpu.VMEM((ROWS, C), f32),
            pltpu.VMEM((6 * W, 128), f32),
            pltpu.SemaphoreType.DMA((4,)),
            pltpu.SemaphoreType.DMA((10,)),
            pltpu.SemaphoreType.DMA((4,)),
        ],
        compiler_params=params,
        name="tail",
    )(
        returned,
        back_h,
        back_l,
        base,
        second_gain.reshape(6, 128),
        second_shift.reshape(6, 128),
        output_bias.reshape(6, 128),
        *far,
        *other,
    )
    return out.reshape(1, W, C)


def solution(mesh):
    fine = Mesh(mesh.devices.reshape(4, 4, 2, 2, 4), AXES)
    chan = AXES[3:]
    placed = (
        P(AXES, None, None),
        P(),
        P(),
        P(chan, None, None, None),
        P(chan, None, None),
        P(chan, None, None, None),
        P(chan, None, None),
        P(),
        P(),
        P(AXES, None, None),
        P(AXES),
        P(),
    )
    return jax.shard_map(
        per_device, mesh=fine, in_specs=placed, out_specs=P(AXES, None, None), check_vma=False
    )
```

```python
import functools

import jax
import jax.numpy as jnp
import numpy as np
from jax import lax
from jax.experimental import pallas as pl
from jax.experimental.pallas import tpu as pltpu
from jax.sharding import Mesh
from jax.sharding import PartitionSpec as P


W = 900
HALF = 450
WP = 512
STEP = 149
PART = 152
KW = 256
H = 256
C = 768
BS = 96
NB = 8
TILE = 2 * PART
ROWS = 3 * TILE
norm_eps = 1e-05
shrink_level = 0.01
AXES = ("zh", "y", "co", "zl", "x")
bf16 = jnp.bfloat16
f32 = jnp.float32


def split_table(values):
    high = values.astype(np.float32).astype(jnp.bfloat16)
    low = (values - high.astype(np.float64)).astype(np.float32).astype(jnp.bfloat16)
    return high, low


def lon_tables():
    k = np.arange(KW).reshape(KW // 2, 2).T
    w = np.arange(HALF)
    angle = 2 * np.pi * (k[:, :, None] * w % W) / W
    forward = np.zeros((2, KW // 2, 2, WP))
    forward[:, :, 0, :HALF] = np.cos(angle)
    forward[:, :, 1, :HALF] = -np.sin(angle)
    forward = forward.reshape(2, KW, WP) * W**-0.5
    factor = np.where(k == 0, 1.0, 2.0)[:, :, None]
    waves = np.stack([np.cos(angle) * factor, -np.sin(angle) * factor], axis=2).reshape(2, KW, HALF) * W**-0.5
    backward = np.stack([waves[:, :, STEP * t : STEP * t + PART].transpose(0, 2, 1) for t in range(3)])
    return split_table(forward), split_table(backward)


def lat_tables():
    m = np.arange(H).reshape(H // 2, 2).T.reshape(H)[:, None]
    h = np.arange(H)[None, :]
    angle = 2 * np.pi * (m * h % H) / H
    cos, sin = np.cos(angle), np.sin(angle)
    forward = np.zeros((2, H, H, 2))
    forward[0, :, :, 0] = cos
    forward[0, :, :, 1] = sin
    forward[1, :, :, 0] = -sin
    forward[1, :, :, 1] = cos
    forward = forward * H**-0.5
    parity = forward.reshape(2, 2, H // 2, H, 2)[:, :, :, : H // 2, :]
    backward = parity.transpose(1, 3, 4, 0, 2).reshape(2, H, H)
    return split_table(forward.reshape(2 * H, 2 * H)), split_table(backward)


def dot(a, b):
    return jnp.dot(a, b, preferred_element_type=f32)


def split(x):
    high = x.astype(bf16)
    return high, (x - high.astype(f32)).astype(bf16)


def row_norm(parts, gain, shift):
    count = len(parts) * 128
    mean = jnp.sum(functools.reduce(jnp.add, parts), axis=-1, keepdims=True) / count
    centered = [p - mean for p in parts]
    square = functools.reduce(jnp.add, [c * c for c in centered])
    scale = lax.rsqrt(jnp.sum(square, axis=-1, keepdims=True) / count + norm_eps)
    return [
        c * scale * gain[j : j + 1, :] + shift[j : j + 1, :]
        for j, c in enumerate(centered)
    ]


def start(copies):
    for copy in copies:
        copy.start()


def pack_filters(refs, out_ref):
    for i, (w_ref, b_ref) in enumerate((refs[:2], refs[2:])):
        top = jnp.concatenate([w_ref[0], w_ref[1]], axis=1)
        bias = jnp.concatenate([b_ref[0:1], b_ref[1:2]], axis=1)
        high = bias.astype(bf16).astype(f32)
        rows = lax.broadcasted_iota(jnp.int32, (16, 2 * BS), 0)
        tail = jnp.where(rows == 0, high, jnp.where(rows == 1, bias - high, 0.0))
        out_ref[i] = jnp.concatenate([top, tail], axis=0).astype(bf16)


def lon_kernel(x_hbm, gain_ref, shift_ref, th_hbm, tl_hbm, f0, f1, f2, f3, *refs):
    modes_ref, base_hbm, pack_ref, x_ref, th, tl, base, high, low, sem, out_sem = refs
    cuts = (0, 960, 1920, 2696, 3664, 4624, 5400)
    loads = [
        pltpu.make_async_copy(x_hbm.at[pl.ds(p, q - p)], x_ref.at[pl.ds(p, q - p)], sem.at[i])
        for i, (p, q) in enumerate(zip(cuts[:-1], cuts[1:]))
    ]
    tables = [pltpu.make_async_copy(th_hbm, th, sem.at[6]), pltpu.make_async_copy(tl_hbm, tl, sem.at[7])]
    start([loads[i] for i in (0, 3, 1, 4, 2, 5)] + tables)
    pack_filters((f0, f1, f2, f3), pack_ref)
    gain = gain_ref[...]
    shift = shift_ref[...]
    for parity in range(2):
        high[parity, 448:WP, :] = jnp.zeros((WP - 448, C), bf16)
        low[parity, 448:WP, :] = jnp.zeros((WP - 448, C), bf16)
    for i, (r, n) in enumerate(((0, 160), (160, 160), (320, 130))):
        loads[i].wait()
        loads[i + 3].wait()
        pairs = []
        for first in (r, HALF + r):
            parts = [x_ref[pl.ds(6 * first + j, n, stride=6), :] for j in range(6)]
            normed = row_norm(parts, gain, shift)
            for j in range(6):
                base[pl.ds(6 * first + j, n, stride=6), :] = normed[j] + parts[j]
            pairs.append(normed)
        for j in range(6):
            lanes = slice(128 * j, 128 * j + 128)
            for parity, value in enumerate((pairs[0][j] + pairs[1][j], pairs[0][j] - pairs[1][j])):
                high[parity, r : r + n, lanes], low[parity, r : r + n, lanes] = split(value)
    store = pltpu.make_async_copy(base, base_hbm, out_sem)
    store.start()
    tables[0].wait()
    tables[1].wait()
    for parity in range(2):
        modes = dot(th[parity], high[parity]) + dot(th[parity], low[parity]) + dot(tl[parity], high[parity])
        modes_ref[128 * parity : 128 * parity + 128] = modes.astype(bf16).reshape(KW // 2, 2, C)
    store.wait()


def mode_kernel(own_ref, x_hbm, fh_hbm, fl_hbm, gh_hbm, gl_hbm, w0, w1, w2, w3, out_ref, x_ref, fh, fl, gh, gl, w_all, zh, zl, sem):
    pairs = [(x_hbm, x_ref), (fh_hbm, fh), (fl_hbm, fl)] + [(w, w_all.at[d]) for d, w in enumerate((w0, w1, w2, w3))]
    pairs += [(gh_hbm, gh), (gl_hbm, gl)]
    copies = [pltpu.make_async_copy(source, target, sem.at[i]) for i, (source, target) in enumerate(pairs)]
    start(copies)
    own = own_ref[0]
    copies[0].wait()
    copies[1].wait()
    x = x_ref[...].reshape(2 * H, C)
    y = dot(fh[...], x)
    copies[2].wait()
    y = y + dot(fl[...], x)
    for copy in copies[3:7]:
        copy.wait()

    def layer(values, slot, i):
        high, low = split(values)
        packed = w_all[jnp.bitwise_and(slot, 3), lax.shift_right_logical(slot, 2), i]
        top = packed[0:BS]
        bottom = jnp.concatenate([-top[:, BS:], top[:, :BS]], axis=1)
        weight = jnp.concatenate([top, bottom], axis=0)
        bias = packed[BS : BS + 16].astype(f32)
        return dot(high, weight) + dot(low, weight) + (bias[0:1] + bias[1:2])

    outs = []
    for b in range(NB):
        slot = jnp.bitwise_xor(own, b)
        lanes = slice(BS * b, BS * b + BS)
        values = jnp.concatenate([y[:H, lanes], y[H:, lanes]], axis=1)
        first = jnp.maximum(layer(values, slot, 0), 0.0)
        second = layer(first, slot, 1)
        outs.append(second - jnp.clip(second, -shrink_level, shrink_level))
    for part in range(2):
        joined = jnp.concatenate([o[:, BS * part : BS * part + BS] for o in outs], axis=1)
        high, low = split(joined)
        for parity in range(2):
            rows = slice(H // 2 * parity, H // 2 * parity + H // 2)
            spot = slice(H // 2 * part, H // 2 * part + H // 2)
            zh[parity, spot, :] = high[rows]
            zl[parity, spot, :] = low[rows]
    copies[7].wait()
    copies[8].wait()
    even, odd = [dot(gh[p], zh[p]) + dot(gh[p], zl[p]) + dot(gl[p], zh[p]) for p in range(2)]
    out_ref[0 : H // 2] = (even + odd).astype(bf16).reshape(H // 2, 2, C)
    out_ref[H // 2 : H] = (even - odd).astype(bf16).reshape(H // 2, 2, C)


def gelu(x):
    return 0.5 * x * (1.0 + lax.erf(x * 0.7071067811865476))


def tail_kernel(x_hbm, th_hbm, tl_hbm, base_hbm, gain_ref, shift_ref, bias_ref, *refs):
    w_hbm, out_hbm = refs[:10], refs[10]
    x_ref, th, tl, base, weights, normed, summed, result, sem, w_sem, out_sem = refs[11:]
    pairs = [(x_hbm, x_ref), (th_hbm, th), (tl_hbm, tl), (base_hbm, base)]
    copies = [pltpu.make_async_copy(source, target, sem.at[i]) for i, (source, target) in enumerate(pairs)]
    w_copies = []
    spot = 0
    for i, w in enumerate(w_hbm):
        w_copies.append(pltpu.make_async_copy(w, weights.at[pl.ds(spot, w.shape[0])], w_sem.at[i]))
        spot += w.shape[0]
    start(copies)
    gain = gain_ref[...]
    shift = shift_ref[...]
    out_bias = bias_ref[...]
    for copy in copies:
        copy.wait()
    start(w_copies)
    x = x_ref[...].reshape(2 * KW, C)
    for t in range(3):
        even, odd = [dot(th[t, p], x[KW * p : KW * p + KW]) + dot(tl[t, p], x[KW * p : KW * p + KW]) for p in range(2)]
        parts = []
        for j in range(6):
            lanes = slice(128 * j, 128 * j + 128)
            near = base[pl.ds(6 * STEP * t + j, PART, stride=6), :]
            far = base[pl.ds(6 * (STEP * t + HALF) + j, PART, stride=6), :]
            parts.append(
                jnp.concatenate([even[:, lanes] + odd[:, lanes] + near, even[:, lanes] - odd[:, lanes] + far], axis=0)
            )
        rows = slice(TILE * t, TILE * t + TILE)
        normed[rows, :] = jnp.concatenate(row_norm(parts, gain, shift), axis=1).astype(bf16)
        for j in range(6):
            summed[rows, 128 * j : 128 * j + 128] = parts[j] + out_bias[j : j + 1, :]

    def out_copy(i, first, last):
        span = pl.ds(first, last - first)
        return pltpu.make_async_copy(result.at[span], out_hbm.at[span], out_sem.at[i])

    outs = [out_copy(i, *c) for i, c in enumerate(((0, 1784), (2704, 4488), (1784, 2704), (4488, 5400)))]

    def tile(t, carry):
        rows = pl.ds(pl.multiple_of(t * TILE, 16), TILE)
        tokens = normed[rows, :]
        acc = summed[rows, :]
        for first, ready in zip(range(0, 32, 8), (w_copies[:2], w_copies[2:5], w_copies[5:7], w_copies[7:])):

            @pl.when(t == 0)
            def _():
                for copy in ready:
                    copy.wait()

            w1 = jnp.concatenate([weights[q, 0:BS, :] for q in range(first, first + 8)], axis=0)
            w2 = jnp.concatenate([weights[q, BS : 2 * BS, :] for q in range(first, first + 8)], axis=0)
            bias = jnp.concatenate(
                [weights[q, 2 * BS : 2 * BS + 16, :].astype(f32)[0:1, 0:BS] for q in range(first, first + 8)], axis=1
            )
            for c in range(3):
                span = slice(256 * c, 256 * c + 256)
                pre = lax.dot_general(tokens, w1[span], (((1,), (1,)), ((), ())), preferred_element_type=f32)
                hidden = gelu(pre + bias[:, span]).astype(bf16)
                acc = acc + dot(hidden, w2[span])
        for j in range(6):
            lanes = slice(128 * j, 128 * j + 128)
            result[pl.ds(6 * STEP * t + j, PART, stride=6), :] = acc[:PART, lanes]
            result[pl.ds(6 * STEP * t + 6 * HALF + j, PART, stride=6), :] = acc[PART:, lanes]

        @pl.when(t == 1)
        def _():
            outs[0].start()
            outs[1].start()

        return carry

    lax.fori_loop(0, 3, tile, 0)
    outs[2].start()
    outs[3].start()
    for copy in outs:
        copy.wait()


def vmem(n):
    return [pl.BlockSpec(memory_space=pltpu.VMEM)] * n


def anywhere(n):
    return [pl.BlockSpec(memory_space=pl.ANY)] * n


params = pltpu.CompilerParams(vmem_limit_bytes=56 * 2**20)


def place(index):
    lat, chan = divmod(index, 8)
    zh, rest = divmod(lat, 8)
    y, core = divmod(rest, 2)
    zl, x = divmod(chan, 4)
    return x, y, zh * 2 + zl, core


def index_of(x, y, z, core):
    return ((z // 2 * 4 + y) * 2 + core) * 8 + z % 2 * 4 + x


def moves(step):
    return [(d, index_of(*step(*place(d)))) for d in range(256)]


def block_moves(bits):
    return [(d, d ^ bits) for d in range(256)]


def near_moves(n):
    return moves(lambda x, y, z, c: (x, (y + n) % 4, z, c) if c == 0 else ((x + n) % 4, y, z, c))


def far_moves(n):
    return moves(lambda x, y, z, c: ((x + n) % 4, y, z, c) if c == 0 else (x, (y + n) % 4, z, c))


core_moves = moves(lambda x, y, z, c: (x, y, z, 1 - c))


def per_device(
    fields,
    first_gain,
    first_shift,
    filter_one,
    filter_one_bias,
    filter_two,
    filter_two_bias,
    second_gain,
    second_shift,
    dense_weights,
    dense_bias,
    output_bias,
):
    (lon_h, lon_l), (back_h, back_l) = lon_tables()
    (lat_h, lat_l), (tal_h, tal_l) = lat_tables()
    shape = jax.ShapeDtypeStruct

    bias_rows = jnp.pad(dense_bias.reshape(1, 1, 12), ((0, 0), (0, 1), (0, C - 12)))
    shard = jnp.concatenate([dense_weights, bias_rows], axis=0)
    copies = jnp.broadcast_to(shard[None], (8,) + shard.shape)
    stacked = lax.all_to_all(copies, ("zh", "zl"), split_axis=0, concat_axis=0, tiled=True)

    modes, base, packed = pl.pallas_call(
        lon_kernel,
        out_shape=(shape((KW, 2, C), bf16), shape((6 * W, 128), f32), shape((2, BS + 16, 2 * BS), bf16)),
        in_specs=anywhere(1) + vmem(2) + anywhere(2) + vmem(4),
        out_specs=(vmem(1)[0], anywhere(1)[0], vmem(1)[0]),
        scratch_shapes=[
            pltpu.VMEM((6 * W, 128), f32),
            pltpu.VMEM((2, KW, WP), bf16),
            pltpu.VMEM((2, KW, WP), bf16),
            pltpu.VMEM((6 * W, 128), f32),
            pltpu.VMEM((2, WP, C), bf16),
            pltpu.VMEM((2, WP, C), bf16),
            pltpu.SemaphoreType.DMA((8,)),
            pltpu.SemaphoreType.DMA,
        ],
        compiler_params=params,
        name="lon",
    )(
        fields.reshape(6 * W, 128),
        first_gain.reshape(6, 128),
        first_shift.reshape(6, 128),
        lon_h,
        lon_l,
        filter_one[0],
        filter_one_bias[0],
        filter_two[0],
        filter_two_bias[0],
    )

    partner = lax.ppermute(packed, AXES, block_moves(4))
    pair = jnp.stack([packed, partner])
    filters = [pair] + [lax.ppermute(pair, AXES, block_moves(b)) for b in range(1, 4)]

    rows_in = stacked[:, :12, 0, :].reshape(BS, C)
    rows_out = stacked[:, :12, 1, :].reshape(BS, C)
    bias_row = jnp.pad(stacked[:, 12, 0, :12].reshape(1, BS), ((0, 15), (0, C - BS)))
    block = jnp.concatenate([rows_in, rows_out, bias_row], axis=0)
    near = [block] + [lax.ppermute(block, AXES, near_moves(n)) for n in (1, -1, 2)]

    moved = lax.all_to_all(modes, AXES, split_axis=0, concat_axis=0, tiled=True)

    group = jnp.stack(near)
    left = lax.ppermute(group, AXES, far_moves(1))
    right = lax.ppermute(group, AXES, far_moves(-1))
    across = [lax.ppermute(left[:2], AXES, far_moves(1)), lax.ppermute(right[2:], AXES, far_moves(-1))]
    far = [group, left, right] + across

    own = lax.axis_index(("zl", "x")).astype(jnp.int32).reshape(1)
    mode_call = pl.pallas_call(
        mode_kernel,
        out_shape=shape((H, 2, C), bf16),
        in_specs=[pl.BlockSpec(memory_space=pltpu.SMEM)] + anywhere(9),
        out_specs=vmem(1)[0],
        scratch_shapes=[pltpu.VMEM((H, 2, C), bf16)]
        + [pltpu.VMEM((2 * H, 2 * H), bf16)] * 2
        + [pltpu.VMEM((2, H, H), bf16)] * 2
        + [
            pltpu.VMEM((4, 2, 2, BS + 16, 2 * BS), bf16),
            pltpu.VMEM((2, H, C), bf16),
            pltpu.VMEM((2, H, C), bf16),
            pltpu.SemaphoreType.DMA((9,)),
        ],
        compiler_params=params,
        name="mode",
    )
    mixed = mode_call(own, moved, lat_h, lat_l, tal_h, tal_l, *filters)

    returned = lax.all_to_all(mixed, AXES, split_axis=0, concat_axis=0, tiled=True)
    other = [lax.ppermute(g, AXES, core_moves) for g in far]

    out = pl.pallas_call(
        tail_kernel,
        out_shape=shape((6 * W, 128), f32),
        in_specs=anywhere(4) + vmem(3) + anywhere(10),
        out_specs=anywhere(1)[0],
        scratch_shapes=[
            pltpu.VMEM((KW, 2, C), bf16),
            pltpu.VMEM((3, 2, PART, KW), bf16),
            pltpu.VMEM((3, 2, PART, KW), bf16),
            pltpu.VMEM((6 * W, 128), f32),
            pltpu.VMEM((32, 2 * BS + 16, C), bf16),
            pltpu.VMEM((ROWS, C), bf16),
            pltpu.VMEM((ROWS, C), f32),
            pltpu.VMEM((6 * W, 128), f32),
            pltpu.SemaphoreType.DMA((4,)),
            pltpu.SemaphoreType.DMA((10,)),
            pltpu.SemaphoreType.DMA((4,)),
        ],
        compiler_params=params,
        name="tail",
    )(
        returned,
        back_h,
        back_l,
        base,
        second_gain.reshape(6, 128),
        second_shift.reshape(6, 128),
        output_bias.reshape(6, 128),
        *far,
        *other,
    )
    return out.reshape(1, W, C)


def solution(mesh):
    fine = Mesh(mesh.devices.reshape(4, 4, 2, 2, 4), AXES)
    chan = AXES[3:]
    placed = (
        P(AXES, None, None),
        P(),
        P(),
        P(chan, None, None, None),
        P(chan, None, None),
        P(chan, None, None, None),
        P(chan, None, None),
        P(),
        P(),
        P(AXES, None, None),
        P(AXES),
        P(),
    )
    return jax.shard_map(
        per_device, mesh=fine, in_specs=placed, out_specs=P(AXES, None, None), check_vma=False
    )
```

```python
import functools

import jax
import jax.numpy as jnp
import numpy as np
from jax import lax
from jax.experimental import pallas as pl
from jax.experimental.pallas import tpu as pltpu
from jax.sharding import Mesh
from jax.sharding import PartitionSpec as P


W = 900
HALF = 450
WP = 512
STEP = 149
PART = 152
KW = 256
H = 256
C = 768
BS = 96
NB = 8
TILE = 2 * PART
ROWS = 3 * TILE
norm_eps = 1e-05
shrink_level = 0.01
AXES = ("zh", "y", "co", "zl", "x")
bf16 = jnp.bfloat16
f32 = jnp.float32


def split_table(values):
    high = values.astype(np.float32).astype(jnp.bfloat16)
    low = (values - high.astype(np.float64)).astype(np.float32).astype(jnp.bfloat16)
    return high, low


def lon_tables():
    k = np.arange(KW).reshape(KW // 2, 2).T
    w = np.arange(HALF)
    angle = 2 * np.pi * (k[:, :, None] * w % W) / W
    forward = np.zeros((2, KW // 2, 2, WP))
    forward[:, :, 0, :HALF] = np.cos(angle)
    forward[:, :, 1, :HALF] = -np.sin(angle)
    forward = forward.reshape(2, KW, WP) * W**-0.5
    factor = np.where(k == 0, 1.0, 2.0)[:, :, None]
    waves = np.stack([np.cos(angle) * factor, -np.sin(angle) * factor], axis=2).reshape(2, KW, HALF) * W**-0.5
    backward = np.stack([waves[:, :, STEP * t : STEP * t + PART].transpose(0, 2, 1) for t in range(3)])
    return split_table(forward), split_table(backward)


def lat_tables():
    m = np.arange(H).reshape(H // 2, 2).T.reshape(H)[:, None]
    h = np.arange(H)[None, :]
    angle = 2 * np.pi * (m * h % H) / H
    cos, sin = np.cos(angle), np.sin(angle)
    forward = np.zeros((2, H, H, 2))
    forward[0, :, :, 0] = cos
    forward[0, :, :, 1] = sin
    forward[1, :, :, 0] = -sin
    forward[1, :, :, 1] = cos
    forward = forward * H**-0.5
    parity = forward.reshape(2, 2, H // 2, H, 2)[:, :, :, : H // 2, :]
    backward = parity.transpose(1, 3, 4, 0, 2).reshape(2, H, H)
    return split_table(forward.reshape(2 * H, 2 * H)), split_table(backward)


def dot(a, b):
    return jnp.dot(a, b, preferred_element_type=f32)


def split(x):
    high = x.astype(bf16)
    return high, (x - high.astype(f32)).astype(bf16)


def row_norm(parts, gain, shift):
    count = len(parts) * 128
    mean = jnp.sum(functools.reduce(jnp.add, parts), axis=-1, keepdims=True) / count
    centered = [p - mean for p in parts]
    square = functools.reduce(jnp.add, [c * c for c in centered])
    scale = lax.rsqrt(jnp.sum(square, axis=-1, keepdims=True) / count + norm_eps)
    return [
        c * scale * gain[j : j + 1, :] + shift[j : j + 1, :]
        for j, c in enumerate(centered)
    ]


def start(copies):
    for copy in copies:
        copy.start()


def pack_filters(refs, out_ref):
    for i, (w_ref, b_ref) in enumerate((refs[:2], refs[2:])):
        top = jnp.concatenate([w_ref[0], w_ref[1]], axis=1)
        bias = jnp.concatenate([b_ref[0:1], b_ref[1:2]], axis=1)
        high = bias.astype(bf16).astype(f32)
        rows = lax.broadcasted_iota(jnp.int32, (16, 2 * BS), 0)
        tail = jnp.where(rows == 0, high, jnp.where(rows == 1, bias - high, 0.0))
        out_ref[i] = jnp.concatenate([top, tail], axis=0).astype(bf16)


def lon_kernel(x_hbm, gain_ref, shift_ref, th_hbm, tl_hbm, f0, f1, f2, f3, *refs):
    modes_ref, base_hbm, pack_ref, x_ref, th, tl, base, high, low, sem, out_sem = refs
    cuts = (0, 960, 1920, 2696, 3664, 4624, 5400)
    loads = [
        pltpu.make_async_copy(x_hbm.at[pl.ds(p, q - p)], x_ref.at[pl.ds(p, q - p)], sem.at[i])
        for i, (p, q) in enumerate(zip(cuts[:-1], cuts[1:]))
    ]
    tables = [pltpu.make_async_copy(th_hbm, th, sem.at[6]), pltpu.make_async_copy(tl_hbm, tl, sem.at[7])]
    start([loads[i] for i in (0, 3, 1, 4, 2, 5)] + tables)
    pack_filters((f0, f1, f2, f3), pack_ref)
    gain = gain_ref[...]
    shift = shift_ref[...]
    for parity in range(2):
        high[parity, 448:WP, :] = jnp.zeros((WP - 448, C), bf16)
        low[parity, 448:WP, :] = jnp.zeros((WP - 448, C), bf16)
    for i, (r, n) in enumerate(((0, 160), (160, 160), (320, 130))):
        loads[i].wait()
        loads[i + 3].wait()
        pairs = []
        for first in (r, HALF + r):
            parts = [x_ref[pl.ds(6 * first + j, n, stride=6), :] for j in range(6)]
            normed = row_norm(parts, gain, shift)
            for j in range(6):
                base[pl.ds(6 * first + j, n, stride=6), :] = normed[j] + parts[j]
            pairs.append(normed)
        for j in range(6):
            lanes = slice(128 * j, 128 * j + 128)
            for parity, value in enumerate((pairs[0][j] + pairs[1][j], pairs[0][j] - pairs[1][j])):
                high[parity, r : r + n, lanes], low[parity, r : r + n, lanes] = split(value)
    store = pltpu.make_async_copy(base, base_hbm, out_sem)
    store.start()
    tables[0].wait()
    tables[1].wait()
    for parity in range(2):
        modes = dot(th[parity], high[parity]) + dot(th[parity], low[parity]) + dot(tl[parity], high[parity])
        modes_ref[128 * parity : 128 * parity + 128] = modes.astype(bf16).reshape(KW // 2, 2, C)
    store.wait()


def mode_kernel(own_ref, x_hbm, fh_hbm, fl_hbm, gh_hbm, gl_hbm, w0, w1, w2, w3, out_ref, x_ref, fh, fl, gh, gl, w_all, zh, zl, sem):
    pairs = [(x_hbm, x_ref), (fh_hbm, fh), (fl_hbm, fl)] + [(w, w_all.at[d]) for d, w in enumerate((w0, w1, w2, w3))]
    pairs += [(gh_hbm, gh), (gl_hbm, gl)]
    copies = [pltpu.make_async_copy(source, target, sem.at[i]) for i, (source, target) in enumerate(pairs)]
    start(copies)
    own = own_ref[0]
    copies[0].wait()
    copies[1].wait()
    x = x_ref[...].reshape(2 * H, C)
    y = dot(fh[...], x)
    copies[2].wait()
    y = y + dot(fl[...], x)
    for copy in copies[3:7]:
        copy.wait()

    def layer(values, slot, i):
        high, low = split(values)
        packed = w_all[jnp.bitwise_and(slot, 3), lax.shift_right_logical(slot, 2), i]
        top = packed[0:BS]
        bottom = jnp.concatenate([-top[:, BS:], top[:, :BS]], axis=1)
        weight = jnp.concatenate([top, bottom], axis=0)
        bias = packed[BS : BS + 16].astype(f32)
        return dot(high, weight) + dot(low, weight) + (bias[0:1] + bias[1:2])

    outs = []
    for b in range(NB):
        slot = jnp.bitwise_xor(own, b)
        lanes = slice(BS * b, BS * b + BS)
        values = jnp.concatenate([y[:H, lanes], y[H:, lanes]], axis=1)
        first = jnp.maximum(layer(values, slot, 0), 0.0)
        second = layer(first, slot, 1)
        outs.append(second - jnp.clip(second, -shrink_level, shrink_level))
    for part in range(2):
        joined = jnp.concatenate([o[:, BS * part : BS * part + BS] for o in outs], axis=1)
        high, low = split(joined)
        for parity in range(2):
            rows = slice(H // 2 * parity, H // 2 * parity + H // 2)
            spot = slice(H // 2 * part, H // 2 * part + H // 2)
            zh[parity, spot, :] = high[rows]
            zl[parity, spot, :] = low[rows]
    copies[7].wait()
    copies[8].wait()
    even, odd = [dot(gh[p], zh[p]) + dot(gh[p], zl[p]) + dot(gl[p], zh[p]) for p in range(2)]
    out_ref[0 : H // 2] = (even + odd).astype(bf16).reshape(H // 2, 2, C)
    out_ref[H // 2 : H] = (even - odd).astype(bf16).reshape(H // 2, 2, C)


def gelu(x):
    return 0.5 * x * (1.0 + lax.erf(x * 0.7071067811865476))


def tail_kernel(x_hbm, th_hbm, tl_hbm, base_hbm, gain_ref, shift_ref, bias_ref, *refs):
    w_hbm, out_hbm = refs[:10], refs[10]
    x_ref, th, tl, base, weights, normed, summed, result, sem, w_sem, out_sem = refs[11:]
    pairs = [(x_hbm, x_ref), (th_hbm, th), (tl_hbm, tl)]
    for p, q in ((0, 912), (2696, 3616), (912, 1808), (3616, 4512), (1808, 2696), (4512, 5400)):
        pairs.append((base_hbm.at[pl.ds(p, q - p)], base.at[pl.ds(p, q - p)]))
    copies = [pltpu.make_async_copy(source, target, sem.at[i]) for i, (source, target) in enumerate(pairs)]
    w_copies = []
    spot = 0
    for i, w in enumerate(w_hbm):
        w_copies.append(pltpu.make_async_copy(w, weights.at[pl.ds(spot, w.shape[0])], w_sem.at[i]))
        spot += w.shape[0]
    start(copies)
    gain = gain_ref[...]
    shift = shift_ref[...]
    out_bias = bias_ref[...]
    for copy in copies[:5]:
        copy.wait()
    start(w_copies)
    x = x_ref[...].reshape(2 * KW, C)
    for t in range(3):
        if t:
            copies[2 * t + 3].wait()
            copies[2 * t + 4].wait()
        even, odd = [dot(th[t, p], x[KW * p : KW * p + KW]) + dot(tl[t, p], x[KW * p : KW * p + KW]) for p in range(2)]
        parts = []
        for j in range(6):
            lanes = slice(128 * j, 128 * j + 128)
            near = base[pl.ds(6 * STEP * t + j, PART, stride=6), :]
            far = base[pl.ds(6 * (STEP * t + HALF) + j, PART, stride=6), :]
            parts.append(
                jnp.concatenate([even[:, lanes] + odd[:, lanes] + near, even[:, lanes] - odd[:, lanes] + far], axis=0)
            )
        rows = slice(TILE * t, TILE * t + TILE)
        normed[rows, :] = jnp.concatenate(row_norm(parts, gain, shift), axis=1).astype(bf16)
        for j in range(6):
            summed[rows, 128 * j : 128 * j + 128] = parts[j] + out_bias[j : j + 1, :]

    def out_copy(i, first, last):
        span = pl.ds(first, last - first)
        return pltpu.make_async_copy(result.at[span], out_hbm.at[span], out_sem.at[i])

    outs = [out_copy(i, *c) for i, c in enumerate(((0, 1784), (2704, 4488), (1784, 2704), (4488, 5400)))]

    def tile(t, carry):
        rows = pl.ds(pl.multiple_of(t * TILE, 16), TILE)
        tokens = normed[rows, :]
        acc = summed[rows, :]
        for first, ready in zip(range(0, 32, 8), (w_copies[:2], w_copies[2:5], w_copies[5:7], w_copies[7:])):

            @pl.when(t == 0)
            def _():
                for copy in ready:
                    copy.wait()

            w1 = jnp.concatenate([weights[q, 0:BS, :] for q in range(first, first + 8)], axis=0)
            w2 = jnp.concatenate([weights[q, BS : 2 * BS, :] for q in range(first, first + 8)], axis=0)
            bias = jnp.concatenate(
                [weights[q, 2 * BS : 2 * BS + 16, :].astype(f32)[0:1, 0:BS] for q in range(first, first + 8)], axis=1
            )
            for c in range(3):
                span = slice(256 * c, 256 * c + 256)
                pre = lax.dot_general(tokens, w1[span], (((1,), (1,)), ((), ())), preferred_element_type=f32)
                hidden = gelu(pre + bias[:, span]).astype(bf16)
                acc = acc + dot(hidden, w2[span])
        for j in range(6):
            lanes = slice(128 * j, 128 * j + 128)
            result[pl.ds(6 * STEP * t + j, PART, stride=6), :] = acc[:PART, lanes]
            result[pl.ds(6 * STEP * t + 6 * HALF + j, PART, stride=6), :] = acc[PART:, lanes]

        @pl.when(t == 1)
        def _():
            outs[0].start()
            outs[1].start()

        return carry

    lax.fori_loop(0, 3, tile, 0)
    outs[2].start()
    outs[3].start()
    for copy in outs:
        copy.wait()


def vmem(n):
    return [pl.BlockSpec(memory_space=pltpu.VMEM)] * n


def anywhere(n):
    return [pl.BlockSpec(memory_space=pl.ANY)] * n


params = pltpu.CompilerParams(vmem_limit_bytes=56 * 2**20)


def place(index):
    lat, chan = divmod(index, 8)
    zh, rest = divmod(lat, 8)
    y, core = divmod(rest, 2)
    zl, x = divmod(chan, 4)
    return x, y, zh * 2 + zl, core


def index_of(x, y, z, core):
    return ((z // 2 * 4 + y) * 2 + core) * 8 + z % 2 * 4 + x


def moves(step):
    return [(d, index_of(*step(*place(d)))) for d in range(256)]


def z_moves(bits):
    return moves(lambda x, y, z, c: (x, y, z ^ bits, c))


def block_moves(bits):
    return [(d, d ^ bits) for d in range(256)]


def near_moves(n):
    return moves(lambda x, y, z, c: (x, (y + n) % 4, z, c) if c == 0 else ((x + n) % 4, y, z, c))


def far_moves(n):
    return moves(lambda x, y, z, c: ((x + n) % 4, y, z, c) if c == 0 else (x, (y + n) % 4, z, c))


core_moves = moves(lambda x, y, z, c: (x, y, z, 1 - c))


def per_device(
    fields,
    first_gain,
    first_shift,
    filter_one,
    filter_one_bias,
    filter_two,
    filter_two_bias,
    second_gain,
    second_shift,
    dense_weights,
    dense_bias,
    output_bias,
):
    (lon_h, lon_l), (back_h, back_l) = lon_tables()
    (lat_h, lat_l), (tal_h, tal_l) = lat_tables()
    shape = jax.ShapeDtypeStruct

    bias_rows = jnp.pad(dense_bias.reshape(1, 1, 12), ((0, 0), (0, 1), (0, C - 12)))
    shard = jnp.concatenate([dense_weights, bias_rows], axis=0)
    shard = lax.optimization_barrier(shard)
    one = lax.ppermute(shard, AXES, z_moves(4))

    modes, base, packed = pl.pallas_call(
        lon_kernel,
        out_shape=(shape((KW, 2, C), bf16), shape((6 * W, 128), f32), shape((2, BS + 16, 2 * BS), bf16)),
        in_specs=anywhere(1) + vmem(2) + anywhere(2) + vmem(4),
        out_specs=(vmem(1)[0], anywhere(1)[0], vmem(1)[0]),
        scratch_shapes=[
            pltpu.VMEM((6 * W, 128), f32),
            pltpu.VMEM((2, KW, WP), bf16),
            pltpu.VMEM((2, KW, WP), bf16),
            pltpu.VMEM((6 * W, 128), f32),
            pltpu.VMEM((2, WP, C), bf16),
            pltpu.VMEM((2, WP, C), bf16),
            pltpu.SemaphoreType.DMA((8,)),
            pltpu.SemaphoreType.DMA,
        ],
        compiler_params=params,
        name="lon",
    )(
        fields.reshape(6 * W, 128),
        first_gain.reshape(6, 128),
        first_shift.reshape(6, 128),
        lon_h,
        lon_l,
        filter_one[0],
        filter_one_bias[0],
        filter_two[0],
        filter_two_bias[0],
    )

    pair_rows = lax.optimization_barrier(jnp.concatenate([shard, one], axis=0))
    two = lax.ppermute(pair_rows, AXES, z_moves(2))
    four_rows = lax.optimization_barrier(jnp.concatenate([pair_rows, two], axis=0))
    four = lax.ppermute(four_rows, AXES, z_moves(1))
    stacked = jnp.concatenate([four_rows, four], axis=0).reshape(8, 13, 2, C)
    partner = lax.ppermute(packed, AXES, block_moves(4))
    pair = jnp.stack([packed, partner])
    filters = [pair] + [lax.ppermute(pair, AXES, block_moves(b)) for b in range(1, 4)]

    rows_in = stacked[:, :12, 0, :].reshape(BS, C)
    rows_out = stacked[:, :12, 1, :].reshape(BS, C)
    bias_row = jnp.pad(stacked[:, 12, 0, :12].reshape(1, BS), ((0, 15), (0, C - BS)))
    block = jnp.concatenate([rows_in, rows_out, bias_row], axis=0)
    near = [block] + [lax.ppermute(block, AXES, near_moves(n)) for n in (1, -1, 2)]

    moved = lax.all_to_all(modes, AXES, split_axis=0, concat_axis=0, tiled=True)

    group = jnp.stack(near)
    left = lax.ppermute(group, AXES, far_moves(1))
    right = lax.ppermute(group, AXES, far_moves(-1))
    across = [lax.ppermute(left[:2], AXES, far_moves(1)), lax.ppermute(right[2:], AXES, far_moves(-1))]
    far = [group, left, right] + across

    own = lax.axis_index(("zl", "x")).astype(jnp.int32).reshape(1)
    mode_call = pl.pallas_call(
        mode_kernel,
        out_shape=shape((H, 2, C), bf16),
        in_specs=[pl.BlockSpec(memory_space=pltpu.SMEM)] + anywhere(9),
        out_specs=vmem(1)[0],
        scratch_shapes=[pltpu.VMEM((H, 2, C), bf16)]
        + [pltpu.VMEM((2 * H, 2 * H), bf16)] * 2
        + [pltpu.VMEM((2, H, H), bf16)] * 2
        + [
            pltpu.VMEM((4, 2, 2, BS + 16, 2 * BS), bf16),
            pltpu.VMEM((2, H, C), bf16),
            pltpu.VMEM((2, H, C), bf16),
            pltpu.SemaphoreType.DMA((9,)),
        ],
        compiler_params=params,
        name="mode",
    )
    mixed = mode_call(own, moved, lat_h, lat_l, tal_h, tal_l, *filters)

    returned = lax.all_to_all(mixed, AXES, split_axis=0, concat_axis=0, tiled=True)
    other = [lax.ppermute(g, AXES, core_moves) for g in far]

    out = pl.pallas_call(
        tail_kernel,
        out_shape=shape((6 * W, 128), f32),
        in_specs=anywhere(4) + vmem(3) + anywhere(10),
        out_specs=anywhere(1)[0],
        scratch_shapes=[
            pltpu.VMEM((KW, 2, C), bf16),
            pltpu.VMEM((3, 2, PART, KW), bf16),
            pltpu.VMEM((3, 2, PART, KW), bf16),
            pltpu.VMEM((6 * W, 128), f32),
            pltpu.VMEM((32, 2 * BS + 16, C), bf16),
            pltpu.VMEM((ROWS, C), bf16),
            pltpu.VMEM((ROWS, C), f32),
            pltpu.VMEM((6 * W, 128), f32),
            pltpu.SemaphoreType.DMA((9,)),
            pltpu.SemaphoreType.DMA((10,)),
            pltpu.SemaphoreType.DMA((4,)),
        ],
        compiler_params=params,
        name="tail",
    )(
        returned,
        back_h,
        back_l,
        base,
        second_gain.reshape(6, 128),
        second_shift.reshape(6, 128),
        output_bias.reshape(6, 128),
        *far,
        *other,
    )
    return out.reshape(1, W, C)


def solution(mesh):
    fine = Mesh(mesh.devices.reshape(4, 4, 2, 2, 4), AXES)
    chan = AXES[3:]
    placed = (
        P(AXES, None, None),
        P(),
        P(),
        P(chan, None, None, None),
        P(chan, None, None),
        P(chan, None, None, None),
        P(chan, None, None),
        P(),
        P(),
        P(AXES, None, None),
        P(AXES),
        P(),
    )
    return jax.shard_map(
        per_device, mesh=fine, in_specs=placed, out_specs=P(AXES, None, None), check_vma=False
    )
```

```python
import functools

import jax
import jax.numpy as jnp
import numpy as np
from jax import lax
from jax.experimental import pallas as pl
from jax.experimental.pallas import tpu as pltpu
from jax.sharding import Mesh
from jax.sharding import PartitionSpec as P


W = 900
HALF = 450
WP = 512
STEP = 149
PART = 152
KW = 256
H = 256
C = 768
BS = 96
NB = 8
BQ = 48
TILE = 2 * PART
ROWS = 3 * TILE
norm_eps = 1e-05
shrink_level = 0.01
AXES = ("zh", "y", "co", "zl", "x")
bf16 = jnp.bfloat16
f32 = jnp.float32


def split_table(values):
    high = values.astype(np.float32).astype(jnp.bfloat16)
    low = (values - high.astype(np.float64)).astype(np.float32).astype(jnp.bfloat16)
    return high, low


def lon_tables():
    k = np.arange(KW).reshape(KW // 2, 2).T
    w = np.arange(HALF)
    angle = 2 * np.pi * (k[:, :, None] * w % W) / W
    forward = np.zeros((2, KW // 2, 2, WP))
    forward[:, :, 0, :HALF] = np.cos(angle)
    forward[:, :, 1, :HALF] = -np.sin(angle)
    forward = forward.reshape(2, KW, WP) * W**-0.5
    factor = np.where(k == 0, 1.0, 2.0)[:, :, None]
    waves = np.stack([np.cos(angle) * factor, -np.sin(angle) * factor], axis=2).reshape(2, KW, HALF) * W**-0.5
    backward = np.stack([waves[:, :, STEP * t : STEP * t + PART].transpose(0, 2, 1) for t in range(3)])
    return split_table(forward), split_table(backward)


def lat_tables():
    m = np.arange(H).reshape(H // 2, 2).T.reshape(H)[:, None]
    h = np.arange(H)[None, :]
    angle = 2 * np.pi * (m * h % H) / H
    cos, sin = np.cos(angle), np.sin(angle)
    forward = np.zeros((2, H, H, 2))
    forward[0, :, :, 0] = cos
    forward[0, :, :, 1] = sin
    forward[1, :, :, 0] = -sin
    forward[1, :, :, 1] = cos
    forward = forward * H**-0.5
    parity = forward.reshape(2, 2, H // 2, H, 2)[:, :, :, : H // 2, :]
    backward = parity.transpose(1, 3, 4, 0, 2).reshape(2, H, H)
    return split_table(forward.reshape(2 * H, 2 * H)), split_table(backward)


def dot(a, b):
    return jnp.dot(a, b, preferred_element_type=f32)


def split(x):
    high = x.astype(bf16)
    return high, (x - high.astype(f32)).astype(bf16)


def row_norm(parts, gain, shift):
    count = len(parts) * 128
    mean = jnp.sum(functools.reduce(jnp.add, parts), axis=-1, keepdims=True) / count
    centered = [p - mean for p in parts]
    square = functools.reduce(jnp.add, [c * c for c in centered])
    scale = lax.rsqrt(jnp.sum(square, axis=-1, keepdims=True) / count + norm_eps)
    return [
        c * scale * gain[j : j + 1, :] + shift[j : j + 1, :]
        for j, c in enumerate(centered)
    ]


def start(copies):
    for copy in copies:
        copy.start()


def pack_filters(refs, out_ref):
    for i, (w_ref, b_ref) in enumerate((refs[:2], refs[2:])):
        top = jnp.concatenate([w_ref[0], w_ref[1]], axis=1)
        bias = jnp.concatenate([b_ref[0:1], b_ref[1:2]], axis=1)
        high = bias.astype(bf16).astype(f32)
        rows = lax.broadcasted_iota(jnp.int32, (16, 2 * BS), 0)
        tail = jnp.where(rows == 0, high, jnp.where(rows == 1, bias - high, 0.0))
        out_ref[i] = jnp.concatenate([top, tail], axis=0).astype(bf16)


def lon_kernel(x_hbm, gain_ref, shift_ref, th_hbm, tl_hbm, f0, f1, f2, f3, *refs):
    modes_ref, base_hbm, pack_ref, x_ref, th, tl, base, high, low, sem, out_sem = refs
    cuts = (0, 960, 1920, 2696, 3664, 4624, 5400)
    loads = [
        pltpu.make_async_copy(x_hbm.at[pl.ds(p, q - p)], x_ref.at[pl.ds(p, q - p)], sem.at[i])
        for i, (p, q) in enumerate(zip(cuts[:-1], cuts[1:]))
    ]
    tables = [pltpu.make_async_copy(th_hbm, th, sem.at[6]), pltpu.make_async_copy(tl_hbm, tl, sem.at[7])]
    start([loads[i] for i in (0, 3, 1, 4, 2, 5)] + tables)
    pack_filters((f0, f1, f2, f3), pack_ref)
    gain = gain_ref[...]
    shift = shift_ref[...]
    for parity in range(2):
        high[parity, 448:WP, :] = jnp.zeros((WP - 448, C), bf16)
        low[parity, 448:WP, :] = jnp.zeros((WP - 448, C), bf16)
    for i, (r, n) in enumerate(((0, 160), (160, 160), (320, 130))):
        loads[i].wait()
        loads[i + 3].wait()
        pairs = []
        for first in (r, HALF + r):
            parts = [x_ref[pl.ds(6 * first + j, n, stride=6), :] for j in range(6)]
            normed = row_norm(parts, gain, shift)
            for j in range(6):
                base[pl.ds(6 * first + j, n, stride=6), :] = normed[j] + parts[j]
            pairs.append(normed)
        for j in range(6):
            lanes = slice(128 * j, 128 * j + 128)
            for parity, value in enumerate((pairs[0][j] + pairs[1][j], pairs[0][j] - pairs[1][j])):
                high[parity, r : r + n, lanes], low[parity, r : r + n, lanes] = split(value)
    store = pltpu.make_async_copy(base, base_hbm, out_sem)
    store.start()
    tables[0].wait()
    tables[1].wait()
    for parity in range(2):
        modes = dot(th[parity], high[parity]) + dot(th[parity], low[parity]) + dot(tl[parity], high[parity])
        modes_ref[128 * parity : 128 * parity + 128] = modes.astype(bf16).reshape(KW // 2, 2, C)
    store.wait()


def mode_kernel(own_ref, x_hbm, fh_hbm, fl_hbm, gh_hbm, gl_hbm, w0, w1, w2, w3, out_ref, x_ref, fh, fl, gh, gl, w_all, zh, zl, sem):
    pairs = [(x_hbm, x_ref), (fh_hbm, fh), (fl_hbm, fl)] + [(w, w_all.at[d]) for d, w in enumerate((w0, w1, w2, w3))]
    pairs += [(gh_hbm, gh), (gl_hbm, gl)]
    copies = [pltpu.make_async_copy(source, target, sem.at[i]) for i, (source, target) in enumerate(pairs)]
    start(copies)
    own = own_ref[0]
    copies[0].wait()
    copies[1].wait()
    x = x_ref[...].reshape(2 * H, C)
    y = dot(fh[...], x)
    copies[2].wait()
    y = y + dot(fl[...], x)
    for copy in copies[3:7]:
        copy.wait()

    def layer(values, slot, i):
        high, low = split(values)
        packed = w_all[jnp.bitwise_and(slot, 3), lax.shift_right_logical(slot, 2), i]
        top = packed[0:BS]
        bottom = jnp.concatenate([-top[:, BS:], top[:, :BS]], axis=1)
        weight = jnp.concatenate([top, bottom], axis=0)
        bias = packed[BS : BS + 16].astype(f32)
        return dot(high, weight) + dot(low, weight) + (bias[0:1] + bias[1:2])

    outs = []
    for b in range(NB):
        slot = jnp.bitwise_xor(own, b)
        lanes = slice(BS * b, BS * b + BS)
        values = jnp.concatenate([y[:H, lanes], y[H:, lanes]], axis=1)
        first = jnp.maximum(layer(values, slot, 0), 0.0)
        second = layer(first, slot, 1)
        outs.append(second - jnp.clip(second, -shrink_level, shrink_level))
    for part in range(2):
        joined = jnp.concatenate([o[:, BS * part : BS * part + BS] for o in outs], axis=1)
        high, low = split(joined)
        for parity in range(2):
            rows = slice(H // 2 * parity, H // 2 * parity + H // 2)
            spot = slice(H // 2 * part, H // 2 * part + H // 2)
            zh[parity, spot, :] = high[rows]
            zl[parity, spot, :] = low[rows]
    copies[7].wait()
    copies[8].wait()
    even, odd = [dot(gh[p], zh[p]) + dot(gh[p], zl[p]) + dot(gl[p], zh[p]) for p in range(2)]
    out_ref[0 : H // 2] = (even + odd).astype(bf16).reshape(H // 2, 2, C)
    out_ref[H // 2 : H] = (even - odd).astype(bf16).reshape(H // 2, 2, C)


def gelu(x):
    return 0.5 * x * (1.0 + lax.erf(x * 0.7071067811865476))


def tail_kernel(x_hbm, th_hbm, tl_hbm, base_hbm, gain_ref, shift_ref, bias_ref, *refs):
    w_hbm, out_hbm = refs[:8], refs[8]
    x_ref, th, tl, base, weights, normed, summed, result, sem, w_sem, out_sem = refs[9:]
    pairs = [(x_hbm, x_ref), (th_hbm, th), (tl_hbm, tl)]
    for p, q in ((0, 912), (2696, 3616), (912, 1808), (3616, 4512), (1808, 2696), (4512, 5400)):
        pairs.append((base_hbm.at[pl.ds(p, q - p)], base.at[pl.ds(p, q - p)]))
    copies = [pltpu.make_async_copy(source, target, sem.at[i]) for i, (source, target) in enumerate(pairs)]
    w_copies = [pltpu.make_async_copy(w, weights.at[pl.ds(8 * i, 8)], w_sem.at[i]) for i, w in enumerate(w_hbm)]
    start(copies)
    gain = gain_ref[...]
    shift = shift_ref[...]
    out_bias = bias_ref[...]
    for copy in copies[:5]:
        copy.wait()
    start(w_copies)
    x = x_ref[...].reshape(2 * KW, C)
    for t in range(3):
        if t:
            copies[2 * t + 3].wait()
            copies[2 * t + 4].wait()
        even, odd = [dot(th[t, p], x[KW * p : KW * p + KW]) + dot(tl[t, p], x[KW * p : KW * p + KW]) for p in range(2)]
        parts = []
        for j in range(6):
            lanes = slice(128 * j, 128 * j + 128)
            near = base[pl.ds(6 * STEP * t + j, PART, stride=6), :]
            far = base[pl.ds(6 * (STEP * t + HALF) + j, PART, stride=6), :]
            parts.append(
                jnp.concatenate([even[:, lanes] + odd[:, lanes] + near, even[:, lanes] - odd[:, lanes] + far], axis=0)
            )
        rows = slice(TILE * t, TILE * t + TILE)
        normed[rows, :] = jnp.concatenate(row_norm(parts, gain, shift), axis=1).astype(bf16)
        for j in range(6):
            summed[rows, 128 * j : 128 * j + 128] = parts[j] + out_bias[j : j + 1, :]

    def out_copy(i, first, last):
        span = pl.ds(first, last - first)
        return pltpu.make_async_copy(result.at[span], out_hbm.at[span], out_sem.at[i])

    outs = [out_copy(i, *c) for i, c in enumerate(((0, 1784), (2704, 4488), (1784, 2704), (4488, 5400)))]

    def tile(t, carry):
        rows = pl.ds(pl.multiple_of(t * TILE, 16), TILE)
        tokens = normed[rows, :]
        acc = summed[rows, :]
        for first in range(0, 64, 16):

            @pl.when(t == 0)
            def _():
                w_copies[first // 8].wait()
                w_copies[first // 8 + 1].wait()

            blocks = range(first, first + 16)
            w1 = jnp.concatenate([weights[q, 0:BQ, :] for q in blocks], axis=0)
            w2 = jnp.concatenate([weights[q, BQ : 2 * BQ, :] for q in blocks], axis=0)
            bias = jnp.concatenate(
                [weights[q, 2 * BQ : 2 * BQ + 16, :].astype(f32)[0:1, 0:BQ] for q in blocks], axis=1
            )
            for c in range(3):
                span = slice(256 * c, 256 * c + 256)
                pre = lax.dot_general(tokens, w1[span], (((1,), (1,)), ((), ())), preferred_element_type=f32)
                hidden = gelu(pre + bias[:, span]).astype(bf16)
                acc = acc + dot(hidden, w2[span])
        for j in range(6):
            lanes = slice(128 * j, 128 * j + 128)
            result[pl.ds(6 * STEP * t + j, PART, stride=6), :] = acc[:PART, lanes]
            result[pl.ds(6 * STEP * t + 6 * HALF + j, PART, stride=6), :] = acc[PART:, lanes]

        @pl.when(t == 1)
        def _():
            outs[0].start()
            outs[1].start()

        return carry

    lax.fori_loop(0, 3, tile, 0)
    outs[2].start()
    outs[3].start()
    for copy in outs:
        copy.wait()


def vmem(n):
    return [pl.BlockSpec(memory_space=pltpu.VMEM)] * n


def anywhere(n):
    return [pl.BlockSpec(memory_space=pl.ANY)] * n


params = pltpu.CompilerParams(vmem_limit_bytes=56 * 2**20)


def place(index):
    lat, chan = divmod(index, 8)
    zh, rest = divmod(lat, 8)
    y, core = divmod(rest, 2)
    zl, x = divmod(chan, 4)
    return x, y, zh * 2 + zl, core


def index_of(x, y, z, core):
    return ((z // 2 * 4 + y) * 2 + core) * 8 + z % 2 * 4 + x


def moves(step):
    return [(d, index_of(*step(*place(d)))) for d in range(256)]


def z_moves(bits):
    return moves(lambda x, y, z, c: (x, y, z ^ bits, c))


def block_moves(bits):
    return [(d, d ^ bits) for d in range(256)]


def near_moves(bits):
    u, v = bits % 4, bits // 4
    return moves(lambda x, y, z, c: (x, y ^ u, z ^ v, c) if c == 0 else (x ^ u, y, z ^ v, c))


def far_moves(n):
    return moves(lambda x, y, z, c: ((x + n) % 4, y, z, c) if c == 0 else (x, (y + n) % 4, z, c))


core_moves = moves(lambda x, y, z, c: (x, y, z, 1 - c))


def per_device(
    fields,
    first_gain,
    first_shift,
    filter_one,
    filter_one_bias,
    filter_two,
    filter_two_bias,
    second_gain,
    second_shift,
    dense_weights,
    dense_bias,
    output_bias,
):
    (lon_h, lon_l), (back_h, back_l) = lon_tables()
    (lat_h, lat_l), (tal_h, tal_l) = lat_tables()
    shape = jax.ShapeDtypeStruct

    bias_rows = jnp.pad(dense_bias.reshape(1, 1, 12), ((0, 0), (0, 1), (0, C - 12)))
    shard = jnp.concatenate([dense_weights, bias_rows], axis=0)
    shard = lax.optimization_barrier(shard)
    one = lax.ppermute(shard, AXES, z_moves(4))

    modes, base, packed = pl.pallas_call(
        lon_kernel,
        out_shape=(shape((KW, 2, C), bf16), shape((6 * W, 128), f32), shape((2, BS + 16, 2 * BS), bf16)),
        in_specs=anywhere(1) + vmem(2) + anywhere(2) + vmem(4),
        out_specs=(vmem(1)[0], anywhere(1)[0], vmem(1)[0]),
        scratch_shapes=[
            pltpu.VMEM((6 * W, 128), f32),
            pltpu.VMEM((2, KW, WP), bf16),
            pltpu.VMEM((2, KW, WP), bf16),
            pltpu.VMEM((6 * W, 128), f32),
            pltpu.VMEM((2, WP, C), bf16),
            pltpu.VMEM((2, WP, C), bf16),
            pltpu.SemaphoreType.DMA((8,)),
            pltpu.SemaphoreType.DMA,
        ],
        compiler_params=params,
        name="lon",
    )(
        fields.reshape(6 * W, 128),
        first_gain.reshape(6, 128),
        first_shift.reshape(6, 128),
        lon_h,
        lon_l,
        filter_one[0],
        filter_one_bias[0],
        filter_two[0],
        filter_two_bias[0],
    )

    pair_rows = lax.optimization_barrier(jnp.concatenate([shard, one], axis=0))
    two = lax.ppermute(pair_rows, AXES, z_moves(2))
    four_rows = lax.optimization_barrier(jnp.concatenate([pair_rows, two], axis=0)).reshape(4, 13, 2, C)
    rows_in = four_rows[:, :12, 0, :].reshape(BQ, C)
    rows_out = four_rows[:, :12, 1, :].reshape(BQ, C)
    bias_row = jnp.pad(four_rows[:, 12, 0, :12].reshape(1, BQ), ((0, 15), (0, C - BQ)))
    block = jnp.concatenate([rows_in, rows_out, bias_row], axis=0)
    partner = lax.ppermute(packed, AXES, block_moves(4))
    pair = jnp.stack([packed, partner])
    filters = [pair] + [lax.ppermute(pair, AXES, block_moves(b)) for b in range(1, 4)]

    near = [block] + [lax.ppermute(block, AXES, near_moves(b)) for b in range(1, 8)]

    moved = lax.all_to_all(modes, AXES, split_axis=0, concat_axis=0, tiled=True)

    group = jnp.stack(near)
    far = [group] + [lax.ppermute(group, AXES, far_moves(n)) for n in (1, -1, 2)]

    own = lax.axis_index(("zl", "x")).astype(jnp.int32).reshape(1)
    mode_call = pl.pallas_call(
        mode_kernel,
        out_shape=shape((H, 2, C), bf16),
        in_specs=[pl.BlockSpec(memory_space=pltpu.SMEM)] + anywhere(9),
        out_specs=vmem(1)[0],
        scratch_shapes=[pltpu.VMEM((H, 2, C), bf16)]
        + [pltpu.VMEM((2 * H, 2 * H), bf16)] * 2
        + [pltpu.VMEM((2, H, H), bf16)] * 2
        + [
            pltpu.VMEM((4, 2, 2, BS + 16, 2 * BS), bf16),
            pltpu.VMEM((2, H, C), bf16),
            pltpu.VMEM((2, H, C), bf16),
            pltpu.SemaphoreType.DMA((9,)),
        ],
        compiler_params=params,
        name="mode",
    )
    mixed = mode_call(own, moved, lat_h, lat_l, tal_h, tal_l, *filters)

    returned = lax.all_to_all(mixed, AXES, split_axis=0, concat_axis=0, tiled=True)
    other = [lax.ppermute(g, AXES, core_moves) for g in far]

    out = pl.pallas_call(
        tail_kernel,
        out_shape=shape((6 * W, 128), f32),
        in_specs=anywhere(4) + vmem(3) + anywhere(8),
        out_specs=anywhere(1)[0],
        scratch_shapes=[
            pltpu.VMEM((KW, 2, C), bf16),
            pltpu.VMEM((3, 2, PART, KW), bf16),
            pltpu.VMEM((3, 2, PART, KW), bf16),
            pltpu.VMEM((6 * W, 128), f32),
            pltpu.VMEM((64, 2 * BQ + 16, C), bf16),
            pltpu.VMEM((ROWS, C), bf16),
            pltpu.VMEM((ROWS, C), f32),
            pltpu.VMEM((6 * W, 128), f32),
            pltpu.SemaphoreType.DMA((9,)),
            pltpu.SemaphoreType.DMA((8,)),
            pltpu.SemaphoreType.DMA((4,)),
        ],
        compiler_params=params,
        name="tail",
    )(
        returned,
        back_h,
        back_l,
        base,
        second_gain.reshape(6, 128),
        second_shift.reshape(6, 128),
        output_bias.reshape(6, 128),
        *far,
        *other,
    )
    return out.reshape(1, W, C)


def solution(mesh):
    fine = Mesh(mesh.devices.reshape(4, 4, 2, 2, 4), AXES)
    chan = AXES[3:]
    placed = (
        P(AXES, None, None),
        P(),
        P(),
        P(chan, None, None, None),
        P(chan, None, None),
        P(chan, None, None, None),
        P(chan, None, None),
        P(),
        P(),
        P(AXES, None, None),
        P(AXES),
        P(),
    )
    return jax.shard_map(
        per_device, mesh=fine, in_specs=placed, out_specs=P(AXES, None, None), check_vma=False
    )
```

```python
import functools

import jax
import jax.numpy as jnp
import numpy as np
from jax import lax
from jax.experimental import pallas as pl
from jax.experimental.pallas import tpu as pltpu
from jax.sharding import Mesh
from jax.sharding import PartitionSpec as P


W = 900
HALF = 450
WP = 512
STEP = 149
PART = 152
KW = 256
H = 256
C = 768
BS = 96
NB = 8
TILE = 2 * PART
ROWS = 3 * TILE
norm_eps = 1e-05
shrink_level = 0.01
AXES = ("zh", "y", "co", "zl", "x")
bf16 = jnp.bfloat16
f32 = jnp.float32


def split_table(values):
    high = values.astype(np.float32).astype(jnp.bfloat16)
    low = (values - high.astype(np.float64)).astype(np.float32).astype(jnp.bfloat16)
    return high, low


def lon_tables():
    k = np.arange(KW).reshape(KW // 2, 2).T
    w = np.arange(HALF)
    angle = 2 * np.pi * (k[:, :, None] * w % W) / W
    forward = np.zeros((2, KW // 2, 2, WP))
    forward[:, :, 0, :HALF] = np.cos(angle)
    forward[:, :, 1, :HALF] = -np.sin(angle)
    forward = forward.reshape(2, KW, WP) * W**-0.5
    factor = np.where(k == 0, 1.0, 2.0)[:, :, None]
    waves = np.stack([np.cos(angle) * factor, -np.sin(angle) * factor], axis=2).reshape(2, KW, HALF) * W**-0.5
    backward = np.stack([waves[:, :, STEP * t : STEP * t + PART].transpose(0, 2, 1) for t in range(3)])
    return split_table(forward), split_table(backward)


def lat_tables():
    m = np.arange(H).reshape(H // 2, 2).T.reshape(H)[:, None]
    h = np.arange(H)[None, :]
    angle = 2 * np.pi * (m * h % H) / H
    cos, sin = np.cos(angle), np.sin(angle)
    forward = np.zeros((2, H, H, 2))
    forward[0, :, :, 0] = cos
    forward[0, :, :, 1] = sin
    forward[1, :, :, 0] = -sin
    forward[1, :, :, 1] = cos
    forward = forward * H**-0.5
    parity = forward.reshape(2, 2, H // 2, H, 2)[:, :, :, : H // 2, :]
    backward = parity.transpose(1, 3, 4, 0, 2).reshape(2, H, H)
    return split_table(forward.reshape(2 * H, 2 * H)), split_table(backward)


def dot(a, b):
    return jnp.dot(a, b, preferred_element_type=f32)


def split(x):
    high = x.astype(bf16)
    return high, (x - high.astype(f32)).astype(bf16)


def row_norm(parts, gain, shift):
    count = len(parts) * 128
    mean = jnp.sum(functools.reduce(jnp.add, parts), axis=-1, keepdims=True) / count
    centered = [p - mean for p in parts]
    square = functools.reduce(jnp.add, [c * c for c in centered])
    scale = lax.rsqrt(jnp.sum(square, axis=-1, keepdims=True) / count + norm_eps)
    return [
        c * scale * gain[j : j + 1, :] + shift[j : j + 1, :]
        for j, c in enumerate(centered)
    ]


def start(copies):
    for copy in copies:
        copy.start()


def pack_filters(refs, out_ref):
    for i, (w_ref, b_ref) in enumerate((refs[:2], refs[2:])):
        top = jnp.concatenate([w_ref[0], w_ref[1]], axis=1)
        bias = jnp.concatenate([b_ref[0:1], b_ref[1:2]], axis=1)
        high = bias.astype(bf16).astype(f32)
        rows = lax.broadcasted_iota(jnp.int32, (16, 2 * BS), 0)
        tail = jnp.where(rows == 0, high, jnp.where(rows == 1, bias - high, 0.0))
        out_ref[i] = jnp.concatenate([top, tail], axis=0).astype(bf16)


def lon_kernel(x_hbm, gain_ref, shift_ref, th_hbm, tl_hbm, f0, f1, f2, f3, *refs):
    modes_ref, base_hbm, pack_ref, x_ref, th, tl, base, high, low, sem, out_sem = refs
    cuts = (0, 960, 1920, 2696, 3664, 4624, 5400)
    loads = [
        pltpu.make_async_copy(x_hbm.at[pl.ds(p, q - p)], x_ref.at[pl.ds(p, q - p)], sem.at[i])
        for i, (p, q) in enumerate(zip(cuts[:-1], cuts[1:]))
    ]
    tables = [pltpu.make_async_copy(th_hbm, th, sem.at[6]), pltpu.make_async_copy(tl_hbm, tl, sem.at[7])]
    start([loads[i] for i in (0, 3, 1, 4, 2, 5)] + tables)
    pack_filters((f0, f1, f2, f3), pack_ref)
    gain = gain_ref[...]
    shift = shift_ref[...]
    for parity in range(2):
        high[parity, 448:WP, :] = jnp.zeros((WP - 448, C), bf16)
        low[parity, 448:WP, :] = jnp.zeros((WP - 448, C), bf16)
    for i, (r, n) in enumerate(((0, 160), (160, 160), (320, 130))):
        loads[i].wait()
        loads[i + 3].wait()
        pairs = []
        for first in (r, HALF + r):
            parts = [x_ref[pl.ds(6 * first + j, n, stride=6), :] for j in range(6)]
            normed = row_norm(parts, gain, shift)
            for j in range(6):
                base[pl.ds(6 * first + j, n, stride=6), :] = normed[j] + parts[j]
            pairs.append(normed)
        for j in range(6):
            lanes = slice(128 * j, 128 * j + 128)
            for parity, value in enumerate((pairs[0][j] + pairs[1][j], pairs[0][j] - pairs[1][j])):
                high[parity, r : r + n, lanes], low[parity, r : r + n, lanes] = split(value)
    store = pltpu.make_async_copy(base, base_hbm, out_sem)
    store.start()
    tables[0].wait()
    tables[1].wait()
    for parity in range(2):
        modes = dot(th[parity], high[parity]) + dot(th[parity], low[parity]) + dot(tl[parity], high[parity])
        modes_ref[128 * parity : 128 * parity + 128] = modes.astype(bf16).reshape(KW // 2, 2, C)
    store.wait()


def mode_kernel(own_ref, x_ref, fh_hbm, fl_hbm, gh_hbm, gl_hbm, w0, w1, w2, w3, out_ref, fh, fl, gh, gl, w_all, zh, zl, sem):
    pairs = [(fh_hbm, fh), (fl_hbm, fl)] + [(w, w_all.at[d]) for d, w in enumerate((w0, w1, w2, w3))]
    pairs += [(gh_hbm, gh), (gl_hbm, gl)]
    copies = [pltpu.make_async_copy(source, target, sem.at[i]) for i, (source, target) in enumerate(pairs)]
    start(copies)
    own = own_ref[0]
    copies[0].wait()
    x = x_ref[...].reshape(2 * H, C)
    y = dot(fh[...], x)
    copies[1].wait()
    y = y + dot(fl[...], x)
    for copy in copies[2:6]:
        copy.wait()

    def layer(values, slot, i):
        high, low = split(values)
        packed = w_all[jnp.bitwise_and(slot, 3), lax.shift_right_logical(slot, 2), i]
        top = packed[0:BS]
        bottom = jnp.concatenate([-top[:, BS:], top[:, :BS]], axis=1)
        weight = jnp.concatenate([top, bottom], axis=0)
        bias = packed[BS : BS + 16].astype(f32)
        return dot(high, weight) + dot(low, weight) + (bias[0:1] + bias[1:2])

    outs = []
    for b in range(NB):
        slot = jnp.bitwise_xor(own, b)
        lanes = slice(BS * b, BS * b + BS)
        values = jnp.concatenate([y[:H, lanes], y[H:, lanes]], axis=1)
        first = jnp.maximum(layer(values, slot, 0), 0.0)
        second = layer(first, slot, 1)
        outs.append(second - jnp.clip(second, -shrink_level, shrink_level))
    for part in range(2):
        joined = jnp.concatenate([o[:, BS * part : BS * part + BS] for o in outs], axis=1)
        high, low = split(joined)
        for parity in range(2):
            rows = slice(H // 2 * parity, H // 2 * parity + H // 2)
            spot = slice(H // 2 * part, H // 2 * part + H // 2)
            zh[parity, spot, :] = high[rows]
            zl[parity, spot, :] = low[rows]
    copies[6].wait()
    copies[7].wait()
    even, odd = [dot(gh[p], zh[p]) + dot(gh[p], zl[p]) + dot(gl[p], zh[p]) for p in range(2)]
    out_ref[0 : H // 2] = (even + odd).astype(bf16).reshape(H // 2, 2, C)
    out_ref[H // 2 : H] = (even - odd).astype(bf16).reshape(H // 2, 2, C)


def gelu(x):
    return 0.5 * x * (1.0 + lax.erf(x * 0.7071067811865476))


def tail_kernel(x_ref, th_hbm, tl_hbm, base_hbm, gain_ref, shift_ref, bias_ref, *refs):
    w_hbm, out_hbm = refs[:10], refs[10]
    th, tl, base, weights, normed, summed, result, sem, w_sem, out_sem = refs[11:]
    pairs = [(th_hbm, th), (tl_hbm, tl)]
    for p, q in ((0, 912), (2696, 3616), (912, 1808), (3616, 4512), (1808, 2696), (4512, 5400)):
        pairs.append((base_hbm.at[pl.ds(p, q - p)], base.at[pl.ds(p, q - p)]))
    copies = [pltpu.make_async_copy(source, target, sem.at[i]) for i, (source, target) in enumerate(pairs)]
    w_copies = []
    spot = 0
    for i, w in enumerate(w_hbm):
        w_copies.append(pltpu.make_async_copy(w, weights.at[pl.ds(spot, w.shape[0])], w_sem.at[i]))
        spot += w.shape[0]
    start(copies)
    gain = gain_ref[...]
    shift = shift_ref[...]
    out_bias = bias_ref[...]
    for copy in copies[:4]:
        copy.wait()
    start(w_copies)
    x = x_ref[...].reshape(2 * KW, C)
    for t in range(3):
        if t:
            copies[2 * t + 2].wait()
            copies[2 * t + 3].wait()
        even, odd = [dot(th[t, p], x[KW * p : KW * p + KW]) + dot(tl[t, p], x[KW * p : KW * p + KW]) for p in range(2)]
        parts = []
        for j in range(6):
            lanes = slice(128 * j, 128 * j + 128)
            near = base[pl.ds(6 * STEP * t + j, PART, stride=6), :]
            far = base[pl.ds(6 * (STEP * t + HALF) + j, PART, stride=6), :]
            parts.append(
                jnp.concatenate([even[:, lanes] + odd[:, lanes] + near, even[:, lanes] - odd[:, lanes] + far], axis=0)
            )
        rows = slice(TILE * t, TILE * t + TILE)
        normed[rows, :] = jnp.concatenate(row_norm(parts, gain, shift), axis=1).astype(bf16)
        for j in range(6):
            summed[rows, 128 * j : 128 * j + 128] = parts[j] + out_bias[j : j + 1, :]

    def out_copy(i, first, last):
        span = pl.ds(first, last - first)
        return pltpu.make_async_copy(result.at[span], out_hbm.at[span], out_sem.at[i])

    outs = [out_copy(i, *c) for i, c in enumerate(((0, 1784), (2704, 4488), (1784, 2704), (4488, 5400)))]

    def tile(t, carry):
        rows = pl.ds(pl.multiple_of(t * TILE, 16), TILE)
        tokens = normed[rows, :]
        acc = summed[rows, :]
        for first, ready in zip(range(0, 32, 8), (w_copies[:2], w_copies[2:5], w_copies[5:7], w_copies[7:])):

            @pl.when(t == 0)
            def _():
                for copy in ready:
                    copy.wait()

            w1 = jnp.concatenate([weights[q, 0:BS, :] for q in range(first, first + 8)], axis=0)
            w2 = jnp.concatenate([weights[q, BS : 2 * BS, :] for q in range(first, first + 8)], axis=0)
            bias = jnp.concatenate(
                [weights[q, 2 * BS : 2 * BS + 16, :].astype(f32)[0:1, 0:BS] for q in range(first, first + 8)], axis=1
            )
            for c in range(3):
                span = slice(256 * c, 256 * c + 256)
                pre = lax.dot_general(tokens, w1[span], (((1,), (1,)), ((), ())), preferred_element_type=f32)
                hidden = gelu(pre + bias[:, span]).astype(bf16)
                acc = acc + dot(hidden, w2[span])
        for j in range(6):
            lanes = slice(128 * j, 128 * j + 128)
            result[pl.ds(6 * STEP * t + j, PART, stride=6), :] = acc[:PART, lanes]
            result[pl.ds(6 * STEP * t + 6 * HALF + j, PART, stride=6), :] = acc[PART:, lanes]

        @pl.when(t == 1)
        def _():
            outs[0].start()
            outs[1].start()

        return carry

    lax.fori_loop(0, 3, tile, 0)
    outs[2].start()
    outs[3].start()
    for copy in outs:
        copy.wait()


def vmem(n):
    return [pl.BlockSpec(memory_space=pltpu.VMEM)] * n


def anywhere(n):
    return [pl.BlockSpec(memory_space=pl.ANY)] * n


params = pltpu.CompilerParams(vmem_limit_bytes=56 * 2**20)


def held(value):
    return pltpu.with_memory_space_constraint(value, pltpu.VMEM)


def place(index):
    lat, chan = divmod(index, 8)
    zh, rest = divmod(lat, 8)
    y, core = divmod(rest, 2)
    zl, x = divmod(chan, 4)
    return x, y, zh * 2 + zl, core


def index_of(x, y, z, core):
    return ((z // 2 * 4 + y) * 2 + core) * 8 + z % 2 * 4 + x


def moves(step):
    return [(d, index_of(*step(*place(d)))) for d in range(256)]


def z_moves(bits):
    return moves(lambda x, y, z, c: (x, y, z ^ bits, c))


def block_moves(bits):
    return [(d, d ^ bits) for d in range(256)]


def near_moves(n):
    return moves(lambda x, y, z, c: (x, y ^ n, z, c) if c == 0 else (x ^ n, y, z, c))


def far_moves(n):
    return moves(lambda x, y, z, c: ((x + n) % 4, y, z, c) if c == 0 else (x, (y + n) % 4, z, c))


core_moves = moves(lambda x, y, z, c: (x, y, z, 1 - c))


def per_device(
    fields,
    first_gain,
    first_shift,
    filter_one,
    filter_one_bias,
    filter_two,
    filter_two_bias,
    second_gain,
    second_shift,
    dense_weights,
    dense_bias,
    output_bias,
):
    (lon_h, lon_l), (back_h, back_l) = lon_tables()
    (lat_h, lat_l), (tal_h, tal_l) = lat_tables()
    shape = jax.ShapeDtypeStruct

    bias_rows = jnp.pad(dense_bias.reshape(1, 1, 12), ((0, 0), (0, 1), (0, C - 12)))
    shard = jnp.concatenate([dense_weights, bias_rows], axis=0)
    shard = lax.optimization_barrier(shard)
    one = lax.ppermute(shard, AXES, z_moves(4))

    modes, base, packed = pl.pallas_call(
        lon_kernel,
        out_shape=(shape((KW, 2, C), bf16), shape((6 * W, 128), f32), shape((2, BS + 16, 2 * BS), bf16)),
        in_specs=anywhere(1) + vmem(2) + anywhere(2) + vmem(4),
        out_specs=(vmem(1)[0], anywhere(1)[0], vmem(1)[0]),
        scratch_shapes=[
            pltpu.VMEM((6 * W, 128), f32),
            pltpu.VMEM((2, KW, WP), bf16),
            pltpu.VMEM((2, KW, WP), bf16),
            pltpu.VMEM((6 * W, 128), f32),
            pltpu.VMEM((2, WP, C), bf16),
            pltpu.VMEM((2, WP, C), bf16),
            pltpu.SemaphoreType.DMA((8,)),
            pltpu.SemaphoreType.DMA,
        ],
        compiler_params=params,
        name="lon",
    )(
        fields.reshape(6 * W, 128),
        first_gain.reshape(6, 128),
        first_shift.reshape(6, 128),
        lon_h,
        lon_l,
        filter_one[0],
        filter_one_bias[0],
        filter_two[0],
        filter_two_bias[0],
    )

    pair_rows = lax.optimization_barrier(jnp.concatenate([shard, one], axis=0))
    two = lax.ppermute(pair_rows, AXES, z_moves(2))
    four_rows = lax.optimization_barrier(jnp.concatenate([pair_rows, two], axis=0))
    four = lax.ppermute(four_rows, AXES, z_moves(1))
    stacked = jnp.concatenate([four_rows, four], axis=0).reshape(8, 13, 2, C)
    partner = lax.ppermute(packed, AXES, block_moves(4))
    pair = jnp.stack([packed, partner])
    filters = [pair] + [lax.ppermute(pair, AXES, block_moves(b)) for b in range(1, 4)]

    rows_in = stacked[:, :12, 0, :].reshape(BS, C)
    rows_out = stacked[:, :12, 1, :].reshape(BS, C)
    bias_row = jnp.pad(stacked[:, 12, 0, :12].reshape(1, BS), ((0, 15), (0, C - BS)))
    block = jnp.concatenate([rows_in, rows_out, bias_row], axis=0)
    near = [block] + [lax.ppermute(block, AXES, near_moves(n)) for n in (1, 3, 2)]

    moved = lax.all_to_all(modes, AXES, split_axis=0, concat_axis=0, tiled=True)

    group = jnp.stack(near)
    left = lax.ppermute(group, AXES, far_moves(1))
    right = lax.ppermute(group, AXES, far_moves(-1))
    across = [lax.ppermute(left[:2], AXES, far_moves(1)), lax.ppermute(right[2:], AXES, far_moves(-1))]
    far = [group, left, right] + across

    own = lax.axis_index(("zl", "x")).astype(jnp.int32).reshape(1)
    mode_call = pl.pallas_call(
        mode_kernel,
        out_shape=shape((H, 2, C), bf16),
        in_specs=[pl.BlockSpec(memory_space=pltpu.SMEM)] + vmem(1) + anywhere(8),
        out_specs=vmem(1)[0],
        scratch_shapes=[pltpu.VMEM((2 * H, 2 * H), bf16)] * 2
        + [pltpu.VMEM((2, H, H), bf16)] * 2
        + [
            pltpu.VMEM((4, 2, 2, BS + 16, 2 * BS), bf16),
            pltpu.VMEM((2, H, C), bf16),
            pltpu.VMEM((2, H, C), bf16),
            pltpu.SemaphoreType.DMA((8,)),
        ],
        compiler_params=params,
        name="mode",
    )
    mixed = mode_call(own, held(moved), lat_h, lat_l, tal_h, tal_l, *filters)

    returned = lax.all_to_all(mixed, AXES, split_axis=0, concat_axis=0, tiled=True)
    other = [lax.ppermute(g, AXES, core_moves) for g in far]

    out = pl.pallas_call(
        tail_kernel,
        out_shape=shape((6 * W, 128), f32),
        in_specs=vmem(1) + anywhere(3) + vmem(3) + anywhere(10),
        out_specs=anywhere(1)[0],
        scratch_shapes=[
            pltpu.VMEM((3, 2, PART, KW), bf16),
            pltpu.VMEM((3, 2, PART, KW), bf16),
            pltpu.VMEM((6 * W, 128), f32),
            pltpu.VMEM((32, 2 * BS + 16, C), bf16),
            pltpu.VMEM((ROWS, C), bf16),
            pltpu.VMEM((ROWS, C), f32),
            pltpu.VMEM((6 * W, 128), f32),
            pltpu.SemaphoreType.DMA((8,)),
            pltpu.SemaphoreType.DMA((10,)),
            pltpu.SemaphoreType.DMA((4,)),
        ],
        compiler_params=params,
        name="tail",
    )(
        held(returned),
        back_h,
        back_l,
        base,
        second_gain.reshape(6, 128),
        second_shift.reshape(6, 128),
        output_bias.reshape(6, 128),
        *far,
        *other,
    )
    return out.reshape(1, W, C)


def solution(mesh):
    fine = Mesh(mesh.devices.reshape(4, 4, 2, 2, 4), AXES)
    chan = AXES[3:]
    placed = (
        P(AXES, None, None),
        P(),
        P(),
        P(chan, None, None, None),
        P(chan, None, None),
        P(chan, None, None, None),
        P(chan, None, None),
        P(),
        P(),
        P(AXES, None, None),
        P(AXES),
        P(),
    )
    return jax.shard_map(
        per_device, mesh=fine, in_specs=placed, out_specs=P(AXES, None, None), check_vma=False
    )
```
